256 devices in a mesh: row: 8 (over y, core), col: 32 (over z, x).
Axes of the slice: x: 4, y: 4, z: 8, core: 2. Of those that a mesh axis runs over, the one named last changes fastest.
Arguments:
- band: float32 [4, 8, 1, 32, 512, 512], P(None, 'row', None, 'col'), as said below
Outputs:
- factored: float32 [4, 8, 1, 32, 512, 512], P(None, 'row', None, 'col')
Inputs may be any that keep to these rules, and one draw needn't show every extreme that they name: band holds the tiles of a symmetric matrix; its diagonal tiles are symmetric positive definite, and those of tile columns 0 and 1 leave every pivot of the steps positive.
All inputs are finite; a program needn't handle non-finite values.
Results may differ from the reference program's by a relative error of at most 0.00015.
Values sent between devices are 32-bit elements; how exact they have to be, the bound alone decides.
No kernel may reach another device: no remote copies, remote signals or barrier semaphores. Data moves between devices by JAX's collectives and lax.ppermute only.
A program may use at most 128 MiB of HBM per device.

```python
import math
import jax
import jax.numpy as jnp
import numpy as np
from jax import lax

TILE = 512
BANDT = 32
STEPS = 2
GRID_ROWS = 8
GRID_COLS = 32
OPD = 4
CPD = 1


def draw_band(key, part):
    grid_rows = BANDT // OPD
    grid_cols = BANDT // CPD
    shape = (OPD, grid_rows, CPD, grid_cols, TILE, TILE)
    slot_idx = jnp.arange(OPD).reshape(-1, 1, 1, 1)
    row_idx = jnp.arange(grid_rows).reshape(1, -1, 1, 1)
    colgrp_idx = jnp.arange(CPD).reshape(1, 1, -1, 1)
    colpos_idx = jnp.arange(grid_cols).reshape(1, 1, 1, -1)
    column_of = colgrp_idx * grid_cols + colpos_idx
    offset_of = slot_idx * grid_rows + (row_idx - column_of) % grid_rows
    keys = jax.random.split(key, 4)
    diag_scale = 2.0 * math.sqrt(TILE)
    support_radius = 0.35
    root_three = math.sqrt(3.0)
    general = jax.random.uniform(keys[0], shape, jnp.float32, -root_three, root_three)
    linking = jax.random.uniform(keys[3], shape, jnp.float32, -0.2 * root_three, 0.2 * root_three)
    points = jax.random.uniform(keys[1], shape[:-2] + (3, TILE), jnp.float32, 0.0, 1.0)
    squared = jnp.zeros(shape, jnp.float32)
    for coord_index in range(3):
        coordinate = points[..., coord_index, :]
        difference = coordinate[..., :, None] - coordinate[..., None, :]
        squared = squared + difference * difference
    distance = jnp.sqrt(squared)
    kernel = jnp.square(jnp.maximum(1.0 - distance / support_radius, 0.0))
    nugget = jax.random.uniform(keys[2], shape[:-1], jnp.float32, 0.5, 1.0)
    eye_mask = jnp.arange(TILE)[:, None] == jnp.arange(TILE)[None, :]
    diag_tile = diag_scale * (kernel + jnp.where(eye_mask, nugget[..., :, None], 0.0))
    is_diag = (offset_of == 0)[..., None, None]
    is_link = ((column_of == 0) & (offset_of == 1))[..., None, None]
    return jnp.where(is_diag, diag_tile, jnp.where(is_link, linking, general))


def setup_inputs(seed: int = 0) -> dict:
    streams_of = jax.random.split(jax.random.key(seed), 2)
    return {
        "band": draw_band(jax.random.fold_in(streams_of[1], 71), 0),
    }


def reference(band):
    grid_rows = GRID_ROWS
    grid_cols = GRID_COLS
    highest = lax.Precision.HIGHEST
    columns = []
    for column_index in range(BANDT):
        offsets = np.arange(BANDT)
        columns.append(band[offsets // grid_rows, (column_index + offsets) % grid_rows, column_index // grid_cols, column_index % grid_cols])
    identity = jnp.eye(TILE, dtype=jnp.float32)
    for step in range(STEPS):
        factor = jnp.linalg.cholesky(columns[step][0])
        inverse = lax.linalg.triangular_solve(factor, identity, left_side=True, lower=True)
        panel = jnp.einsum('dab,cb->dac', columns[step], inverse, precision=highest)
        panel = panel.at[0].set(factor)
        columns[step] = panel
        for target in range(step + 1, BANDT):
            count = step + BANDT - target
            update = jnp.einsum('dab,cb->dac', panel[target - step:target - step + count], panel[target - step], precision=highest)
            columns[target] = columns[target].at[:count].add(-update)
    stacked = jnp.stack(columns)
    slot_idx, row_idx, colgrp_idx, colpos_idx = np.meshgrid(np.arange(OPD), np.arange(grid_rows), np.arange(CPD), np.arange(grid_cols), indexing='ij')
    column_of = colgrp_idx * grid_cols + colpos_idx
    offset_of = slot_idx * grid_rows + (row_idx - column_of) % grid_rows
    return stacked[column_of, offset_of]
```

```python
import jax
import jax.numpy as jnp
from jax import lax
from jax.experimental import pallas as pl
from jax.experimental.pallas import tpu as pltpu
from jax.sharding import PartitionSpec as P


TILE=512; NB=128; NBLK=4
HI=lax.Precision.HIGHEST

def block_factor(s_ref, x_ref, b):
    off = pl.multiple_of(b*NB, NB)
    s=[s_ref[pl.ds(off+8*i,8), pl.ds(off,NB)] for i in range(16)]
    rows=lax.broadcasted_iota(jnp.int32,(8,NB),0)
    cols=lax.broadcasted_iota(jnp.int32,(8,NB),1)
    x=[jnp.where(cols==rows+8*i,1.0,0.0).astype(jnp.float32) for i in range(16)]
    def lane(v,c): return jnp.broadcast_to(v[:,c:c+1],(8,NB))
    def sub(v,j): return jnp.broadcast_to(v[j:j+1,:],(8,NB))
    for g in range(16):
        c=[lane(s[g],8*g+k) for k in range(8)]
        inv=[None]*8; q=[[None]*8 for _ in range(8)]; sr=[None]*8; xr=[None]*8
        for k in range(8):
            inv[k]=1.0/sub(c[k],k)
            sr[k]=sub(s[g],k); xr[k]=sub(x[g],k)
            if k<7:
                t=jnp.where(rows>k,c[k]*inv[k],0.0)
                for k2 in range(k+1,8):
                    q[k][k2]=sub(c[k2],k)
                    c[k2]=c[k2]-t*q[k][k2]
                s[g]=s[g]-t*sr[k]
                x[g]=x[g]-t*xr[k]
        for i in range(g+1,16):
            ci=[lane(s[i],8*g+k) for k in range(8)]
            for k in range(8):
                t=ci[k]*inv[k]
                for k2 in range(k+1,8):
                    ci[k2]=ci[k2]-t*q[k][k2]
                s[i]=s[i]-t*sr[k]
                x[i]=x[i]-t*xr[k]
    return s,x

def kernel(a_ref, l_ref, v_ref, w_ref, u_ref):
    w_ref[...]=a_ref[...]
    v_ref[...]=jnp.zeros((TILE,TILE),jnp.float32)
    l_ref[...]=jnp.zeros((TILE,TILE),jnp.float32)
    rows=lax.broadcasted_iota(jnp.int32,(NB,NB),0)
    cols=lax.broadcasted_iota(jnp.int32,(NB,NB),1)
    def step(b,carry):
        s,x=block_factor(w_ref,v_ref,b)
        sb=jnp.concatenate(s,0); xb=jnp.concatenate(x,0)
        d=jnp.sum(jnp.where(rows==cols,sb,0.0),axis=1,keepdims=True)
        r=lax.rsqrt(d)
        ub=jnp.where(cols>=rows,sb*r,0.0)
        vb=jnp.where(cols<=rows,xb*r,0.0)
        lb=ub.T
        off=pl.multiple_of(b*NB,NB)
        for bb in range(NBLK):
            @pl.when(b==bb)
            def _(bb=bb):
                o=bb*NB
                l_ref[o:o+NB,o:o+NB]=lb
                if bb>0:
                    vleft=jnp.dot(vb,v_ref[o:o+NB,:o],precision=HI,preferred_element_type=jnp.float32)
                    v_ref[o:o+NB,:o]=vleft
                v_ref[o:o+NB,o:o+NB]=vb
                if bb<NBLK-1:
                    e=o+NB
                    lp=lax.dot_general(w_ref[e:,o:e],vb,(((1,),(1,)),((),())),precision=HI,preferred_element_type=jnp.float32)
                    l_ref[e:,o:e]=lp
                    w_ref[e:,e:]-=lax.dot_general(lp,lp,(((1,),(1,)),((),())),precision=HI,preferred_element_type=jnp.float32)
                    v_ref[e:,:e]-=jnp.dot(lp,v_ref[o:e,:e],precision=HI,preferred_element_type=jnp.float32)
        return carry
    lax.fori_loop(0,NBLK,step,0)

def chol_inv(a):
    return pl.pallas_call(kernel,
        out_shape=(jax.ShapeDtypeStruct((TILE,TILE),jnp.float32),)*2,
        in_specs=[pl.BlockSpec(memory_space=pltpu.VMEM)],
        out_specs=(pl.BlockSpec(memory_space=pltpu.VMEM),)*2,
        scratch_shapes=[pltpu.VMEM((TILE,TILE),jnp.float32),pltpu.VMEM((NB,NB),jnp.float32)],
        name="chol_inv")(a)


BANDT = 32
ROWS = 8
COLS = 32
AX = ("row", "col")
HIGHEST = lax.Precision.HIGHEST
HIGH = lax.Precision.HIGH


def lin(r, c):
    return (r % ROWS) * COLS + c % COLS


def zx(z, x):
    return (z % 8) * 4 + x % 4


def permute(x, pairs):
    return lax.ppermute(x, AX, [(lin(*a), lin(*b)) for a, b in pairs])


def ordered(pieces, start):
    n = len(pieces)
    stacked = jnp.stack(pieces + pieces)
    return lax.dynamic_slice_in_dim(stacked, (n - start) % n, n, 0)


def row_gather(piece, row):
    y, core = row // 2, row % 2
    same = [piece] + [
        permute(piece, [((r, c), (r - 2 * m, c)) for r in range(ROWS) for c in range(COLS)])
        for m in range(1, 4)
    ]
    mine = ordered(same, y)
    other = permute(mine, [((r, c), (r ^ 1, c)) for r in range(ROWS) for c in range(COLS)])
    even = jnp.where(core == 0, mine, other)
    odd = jnp.where(core == 0, other, mine)
    both = jnp.stack([even, odd], axis=1)
    return both.reshape((ROWS,) + piece.shape)


def broadcast_all(x, root_row, row, z, xpos):
    n, tile, _ = x.shape
    part = tile // ROWS
    x = x.reshape(n, ROWS, part, tile)
    piece = jnp.where(row == root_row, x[:, root_row], 0.0)
    for k in range(1, ROWS):
        to = (root_row + k) % ROWS
        piece = piece + permute(x[:, to], [((root_row, 0), (to, 0))])
    got = jnp.where(xpos == 0, piece, 0.0)
    for dx in range(1, 4):
        got = got + permute(piece, [((r, 0), (r, dx)) for r in range(ROWS)])
    fine = got.reshape(n, 8, part // 8, tile)
    mine = jnp.where(z == 0, fine[:, 0], 0.0)
    for dz in range(1, 8):
        mine = mine + permute(fine[:, dz], [((r, c), (r, zx(dz, c))) for r in range(ROWS) for c in range(4)])
    ring = [mine] + [
        permute(mine, [((r, zx(a, b)), (r, zx(a - m, b))) for r in range(ROWS) for a in range(8) for b in range(4)])
        for m in range(1, 8)
    ]
    piece = jnp.swapaxes(ordered(ring, z), 0, 1).reshape(n, part, tile)
    full = row_gather(piece, row)
    return jnp.swapaxes(full, 0, 1).reshape(n, tile, tile)


def shards(band):
    slots, _, _, _, tile, _ = band.shape
    part = tile // ROWS
    row = lax.axis_index("row")
    col = lax.axis_index("col")
    z, xpos = col // 4, col % 4
    local = band.reshape(slots, tile, tile)
    a00 = broadcast_all(local[:1], 0, row, z, xpos)[0]
    first = permute(local[0], [((1, 1), (1, 0))])
    pair = broadcast_all(jnp.stack([local[0], first]), 1, row, z, xpos)
    a10, a11 = pair[0], pair[1]

    flat = local.reshape(COLS, part, tile)
    flat = jnp.where(col == 1, jnp.roll(flat, -1, axis=0), flat)
    p0 = jnp.where(col == 0, flat[0], 0.0)
    p1 = jnp.where(col == 1, flat[0], 0.0)
    for k in range(1, COLS):
        got = permute(flat[k], [((r, 0), (r, k)) for r in range(ROWS)] + [((r, 1), (r, k + 1)) for r in range(ROWS)])
        p0 = p0 + jnp.where(col == k, got, 0.0)
        p1 = p1 + jnp.where(col == (k + 1) % COLS, got, 0.0)
    panels = lax.all_gather(jnp.stack([p0, p1]), "col")
    raw0 = panels[:, 0].reshape(slots, tile, tile)
    raw1 = panels[:, 1].reshape(slots, tile, tile)

    t0 = lax.dynamic_index_in_dim(raw0, jnp.minimum(col // 8, 3), 0, keepdims=False)
    t1 = lax.dynamic_index_in_dim(raw1, jnp.clip((col - 1) // 8, 0, 3), 0, keepdims=False)
    both = jnp.stack([t0, t1]).reshape(2, ROWS, part, tile)
    own = lax.dynamic_index_in_dim(both, row, 1, keepdims=False)
    piece = jnp.where(row == col % ROWS, own, 0.0)
    for k in range(1, ROWS):
        send = lax.dynamic_index_in_dim(both, (row + k) % ROWS, 1, keepdims=False)
        piece = piece + permute(send, [((c, c), (c + k, c)) for c in range(COLS)])
    full = jnp.swapaxes(row_gather(piece, row), 0, 1).reshape(2, tile, tile)
    t0, t1 = full[0], full[1]

    def times_t(a, b, precision=HIGH):
        return jnp.einsum("...ab,cb->...ac", a, b, precision=precision)

    factor0, inverse0 = chol_inv(a00)
    p01 = times_t(a10, inverse0, HIGHEST)
    factor1, inverse1 = chol_inv(a11 - times_t(p01, p01, HIGHEST))

    rows_here = col + (row - col) % ROWS + ROWS * jnp.arange(slots, dtype=jnp.int32)
    live0 = (rows_here <= BANDT - 1)[:, None, None]
    live1 = (rows_here <= BANDT)[:, None, None]
    s0 = jnp.take(raw0, jnp.clip(rows_here // ROWS, 0, slots - 1), axis=0)
    s1 = jnp.take(raw1, jnp.clip((rows_here - 1) // ROWS, 0, slots - 1), axis=0)
    panel0 = jnp.where(live0, times_t(s0, inverse0), 0.0)
    panel0_t = times_t(t0, inverse0)
    panel1 = jnp.where(live1, times_t(s1 - times_t(panel0, p01), inverse1), 0.0)
    panel1_t = times_t(t1 - times_t(panel0_t, p01), inverse1)
    updated = local - times_t(panel0, panel0_t) - times_t(panel1, panel1_t)
    is0 = (rows_here == 0)[:, None, None]
    is1 = (rows_here == 1)[:, None, None]
    out = jnp.where(
        col == 0,
        jnp.where(is0, factor0, panel0),
        jnp.where(col == 1, jnp.where(is1, factor1, panel1), updated),
    )
    return out.reshape(band.shape)


def solution(mesh):
    spec = P(None, "row", None, "col", None, None)
    return jax.shard_map(shards, mesh=mesh, in_specs=(spec,), out_specs=spec, check_vma=False)
```

```python
import jax
import jax.numpy as jnp
from jax import lax
from jax.experimental import pallas as pl
from jax.experimental.pallas import tpu as pltpu
from jax.sharding import PartitionSpec as P


TILE=512; NB=128; NBLK=4
HI=lax.Precision.HIGHEST

def block_factor(s_ref, x_ref, b):
    off = pl.multiple_of(b*NB, NB)
    s=[s_ref[pl.ds(off+8*i,8), pl.ds(off,NB)] for i in range(16)]
    rows=lax.broadcasted_iota(jnp.int32,(8,NB),0)
    cols=lax.broadcasted_iota(jnp.int32,(8,NB),1)
    x=[jnp.where(cols==rows+8*i,1.0,0.0).astype(jnp.float32) for i in range(16)]
    def lane(v,c): return jnp.broadcast_to(v[:,c:c+1],(8,NB))
    def sub(v,j): return jnp.broadcast_to(v[j:j+1,:],(8,NB))
    for g in range(16):
        c=[lane(s[g],8*g+k) for k in range(8)]
        inv=[None]*8; q=[[None]*8 for _ in range(8)]; sr=[None]*8; xr=[None]*8
        for k in range(8):
            inv[k]=1.0/sub(c[k],k)
            sr[k]=sub(s[g],k); xr[k]=sub(x[g],k)
            if k<7:
                t=jnp.where(rows>k,c[k]*inv[k],0.0)
                for k2 in range(k+1,8):
                    q[k][k2]=sub(c[k2],k)
                    c[k2]=c[k2]-t*q[k][k2]
                s[g]=s[g]-t*sr[k]
                x[g]=x[g]-t*xr[k]
        for i in range(g+1,16):
            ci=[lane(s[i],8*g+k) for k in range(8)]
            for k in range(8):
                t=ci[k]*inv[k]
                for k2 in range(k+1,8):
                    ci[k2]=ci[k2]-t*q[k][k2]
                s[i]=s[i]-t*sr[k]
                x[i]=x[i]-t*xr[k]
    return s,x

def kernel(a_ref, l_ref, v_ref, w_ref, u_ref):
    w_ref[...]=a_ref[...]
    v_ref[...]=jnp.zeros((TILE,TILE),jnp.float32)
    l_ref[...]=jnp.zeros((TILE,TILE),jnp.float32)
    rows=lax.broadcasted_iota(jnp.int32,(NB,NB),0)
    cols=lax.broadcasted_iota(jnp.int32,(NB,NB),1)
    def step(b,carry):
        s,x=block_factor(w_ref,v_ref,b)
        sb=jnp.concatenate(s,0); xb=jnp.concatenate(x,0)
        d=jnp.sum(jnp.where(rows==cols,sb,0.0),axis=1,keepdims=True)
        r=lax.rsqrt(d)
        ub=jnp.where(cols>=rows,sb*r,0.0)
        vb=jnp.where(cols<=rows,xb*r,0.0)
        lb=ub.T
        off=pl.multiple_of(b*NB,NB)
        for bb in range(NBLK):
            @pl.when(b==bb)
            def _(bb=bb):
                o=bb*NB
                l_ref[o:o+NB,o:o+NB]=lb
                if bb>0:
                    vleft=jnp.dot(vb,v_ref[o:o+NB,:o],precision=HI,preferred_element_type=jnp.float32)
                    v_ref[o:o+NB,:o]=vleft
                v_ref[o:o+NB,o:o+NB]=vb
                if bb<NBLK-1:
                    e=o+NB
                    lp=lax.dot_general(w_ref[e:,o:e],vb,(((1,),(1,)),((),())),precision=HI,preferred_element_type=jnp.float32)
                    l_ref[e:,o:e]=lp
                    w_ref[e:,e:]-=lax.dot_general(lp,lp,(((1,),(1,)),((),())),precision=HI,preferred_element_type=jnp.float32)
                    v_ref[e:,:e]-=jnp.dot(lp,v_ref[o:e,:e],precision=HI,preferred_element_type=jnp.float32)
        return carry
    lax.fori_loop(0,NBLK,step,0)

def chol_inv(a):
    return pl.pallas_call(kernel,
        out_shape=(jax.ShapeDtypeStruct((TILE,TILE),jnp.float32),)*2,
        in_specs=[pl.BlockSpec(memory_space=pltpu.VMEM)],
        out_specs=(pl.BlockSpec(memory_space=pltpu.VMEM),)*2,
        scratch_shapes=[pltpu.VMEM((TILE,TILE),jnp.float32),pltpu.VMEM((NB,NB),jnp.float32)],
        name="chol_inv")(a)


BANDT = 32
ROWS = 8
COLS = 32
AX = ("row", "col")
HIGHEST = lax.Precision.HIGHEST
HIGH = lax.Precision.HIGH


def lin(r, c):
    return (r % ROWS) * COLS + c % COLS


def zx(z, x):
    return (z % 8) * 4 + x % 4


def permute(x, pairs):
    return lax.ppermute(x, AX, [(lin(*a), lin(*b)) for a, b in pairs])


EVERY = [(r, z, x) for r in range(ROWS) for z in range(8) for x in range(4)]


def core_swap(v):
    return permute(v, [((r, zx(z, x)), (r ^ 1, zx(z, x))) for r, z, x in EVERY])


def y_shift(v, k):
    return permute(v, [((r, zx(z, x)), (r + 2 * k, zx(z, x))) for r, z, x in EVERY])


def x_shift(v, k):
    return permute(v, [((r, zx(z, x)), (r, zx(z, x + k))) for r, z, x in EVERY])


def z_shift(v, k):
    return permute(v, [((r, zx(z, x)), (r, zx(z + k, x))) for r, z, x in EVERY])


def x_deal(v, k):
    return permute(v, [((r, zx(z, x)), (r, zx(z, x + k))) for r, z, x in EVERY if x < 2])


def z_deal(v, k):
    return permute(v, [((r, zx(0, x)), (r, zx(k, x))) for r, z, x in EVERY if z == 0])


def ordered(pieces, start):
    n = len(pieces)
    stacked = jnp.stack(pieces + pieces)
    return lax.dynamic_slice_in_dim(stacked, (n - start) % n, n, 0)


def pick(choices):
    total = None
    for cond, v in choices:
        v = jnp.where(cond, v, 0.0)
        total = v if total is None else total + v
    return total


def row_scatter(x, root_y, root_core, y, core):
    n, tile, _ = x.shape
    x = x.reshape(n, 4, 2, tile // ROWS, tile)
    same = jnp.where(core == 0, x[:, :, 0], x[:, :, 1])
    away = jnp.where(core == 0, x[:, :, 1], x[:, :, 0])
    got = core_swap(away)
    mine = jnp.where(core == root_core, same, got)
    parts = [(y == root_y, lax.dynamic_index_in_dim(mine, y, 1, keepdims=False))]
    for k in range(1, 4):
        send = lax.dynamic_index_in_dim(mine, (y + k) % 4, 1, keepdims=False)
        parts.append((y == (root_y + k) % 4, y_shift(send, k)))
    return pick(parts)


def row_gather(piece, y, core):
    mine = ordered([piece] + [y_shift(piece, 4 - m) for m in range(1, 4)], y)
    other = core_swap(mine)
    even = jnp.where(core == 0, mine, other)
    odd = jnp.where(core == 0, other, mine)
    full = jnp.stack([even, odd], axis=1)
    n, part, tile = piece.shape
    full = full.reshape(ROWS, n, part, tile)
    return jnp.swapaxes(full, 0, 1).reshape(n, tile, tile)


def broadcast_all(v, y, core, z, x):
    n, tile, _ = v.shape
    part = tile // ROWS
    piece = row_scatter(v, 0, 0, y, core)
    piece = pick([(x == 0, piece)] + [(x == k, x_shift(piece, k)) for k in range(1, 4)])
    fine = piece.reshape(n, 8, part // 8, tile)
    mine = pick([(z == 0, fine[:, 0])] + [(z == k, z_shift(fine[:, k], k)) for k in range(1, 8)])
    ring = ordered([mine] + [z_shift(mine, 8 - m) for m in range(1, 8)], z)
    piece = jnp.swapaxes(ring, 0, 1).reshape(n, part, tile)
    return row_gather(piece, y, core)


def shards(band):
    slots, _, _, _, tile, _ = band.shape
    part = tile // ROWS
    row = lax.axis_index("row")
    col = lax.axis_index("col")
    z, x = col // 4, col % 4
    y, core = row // 2, row % 2
    local = band.reshape(slots, tile, tile)
    partner = core_swap(local[0])
    a11 = permute(partner, [((0, 1), (0, 0))])
    a00 = broadcast_all(local[:1], y, core, z, x)[0]
    pair = broadcast_all(jnp.stack([partner, a11]), y, core, z, x)
    a10, a11 = pair[0], pair[1]

    halves = local.reshape(2, 8, 4, part // 2, tile)
    top, low = halves[0], halves[1]

    def deal_x(v):
        first, second = [(x == 0, v[..., 0, :, :])], [(x == 1, v[..., 1, :, :])]
        for k in range(1, 4):
            send = jnp.where(x == 0, v[..., k, :, :], v[..., (k + 1) % 4, :, :])
            got = x_deal(send, k)
            first.append((x == k, got))
            second.append((x == (k + 1) % 4, got))
        return jnp.stack([pick(first), pick(second)])

    def deal_z(v):
        return pick([(z == 0, v[0])] + [(z == k, z_deal(v[k], k)) for k in range(1, 8)])

    low = deal_x(deal_z(low))
    top = deal_z(jnp.swapaxes(deal_x(top), 0, 1))
    panels = lax.all_gather(jnp.stack([top, low]), "col")
    raw0 = jnp.swapaxes(panels[:, :, 0], 0, 1).reshape(slots, tile, tile)
    raw1 = jnp.swapaxes(panels[:, :, 1], 0, 1).reshape(slots, tile, tile)

    t0 = lax.dynamic_index_in_dim(raw0, jnp.minimum(col // 8, 3), 0, keepdims=False)
    t1 = lax.dynamic_index_in_dim(raw1, jnp.clip((col - 1) // 8, 0, 3), 0, keepdims=False)
    root = col % ROWS
    piece = row_scatter(jnp.stack([t0, t1]), root // 2, root % 2, y, core)
    full = row_gather(piece, y, core)
    t0, t1 = full[0], full[1]

    def times_t(a, b, precision=HIGH):
        return jnp.einsum("...ab,cb->...ac", a, b, precision=precision)

    factor0, inverse0 = chol_inv(a00)
    p01 = times_t(a10, inverse0, HIGHEST)
    factor1, inverse1 = chol_inv(a11 - times_t(p01, p01, HIGHEST))

    rows_here = col + (row - col) % ROWS + ROWS * jnp.arange(slots, dtype=jnp.int32)
    live0 = (rows_here <= BANDT - 1)[:, None, None]
    live1 = (rows_here <= BANDT)[:, None, None]
    s0 = jnp.take(raw0, jnp.clip(rows_here // ROWS, 0, slots - 1), axis=0)
    s1 = jnp.take(raw1, jnp.clip((rows_here - 1) // ROWS, 0, slots - 1), axis=0)
    panel0 = jnp.where(live0, times_t(s0, inverse0), 0.0)
    panel0_t = times_t(t0, inverse0)
    panel1 = jnp.where(live1, times_t(s1 - times_t(panel0, p01), inverse1), 0.0)
    panel1_t = times_t(t1 - times_t(panel0_t, p01), inverse1)
    updated = local - times_t(panel0, panel0_t) - times_t(panel1, panel1_t)
    is0 = (rows_here == 0)[:, None, None]
    is1 = (rows_here == 1)[:, None, None]
    out = jnp.where(
        col == 0,
        jnp.where(is0, factor0, panel0),
        jnp.where(col == 1, jnp.where(is1, factor1, panel1), updated),
    )
    return out.reshape(band.shape)


def solution(mesh):
    spec = P(None, "row", None, "col", None, None)
    return jax.shard_map(shards, mesh=mesh, in_specs=(spec,), out_specs=spec, check_vma=False)
```

```python
import jax
import jax.numpy as jnp
from jax import lax
from jax.experimental import pallas as pl
from jax.experimental.pallas import tpu as pltpu
from jax.sharding import PartitionSpec as P


TILE = 512
NB = 128
NBLK = TILE // NB
PART = TILE // 8
HIGHEST = lax.Precision.HIGHEST
VMEM = pl.BlockSpec(memory_space=pltpu.VMEM)
SMEM = pl.BlockSpec(memory_space=pltpu.SMEM)
F32 = jnp.float32


def square(n=1):
    return (jax.ShapeDtypeStruct((TILE, TILE), F32),) * n


def times_t(a, b):
    return lax.dot_general(a, b, (((1,), (1,)), ((), ())), precision=HIGHEST, preferred_element_type=F32)


def block_factor(s):
    rows = lax.broadcasted_iota(jnp.int32, (8, NB), 0)
    cols = lax.broadcasted_iota(jnp.int32, (8, NB), 1)
    x = [jnp.where(cols == rows + 8 * i, 1.0, 0.0).astype(F32) for i in range(16)]

    def lane(v, c):
        return jnp.broadcast_to(v[:, c : c + 1], (8, NB))

    def sub(v, j):
        return jnp.broadcast_to(v[j : j + 1, :], (8, NB))

    for g in range(16):
        c = [lane(s[g], 8 * g + k) for k in range(8)]
        inv, q, sr, xr = [None] * 8, [[None] * 8 for _ in range(8)], [None] * 8, [None] * 8
        for k in range(8):
            inv[k] = 1.0 / sub(c[k], k)
            sr[k], xr[k] = sub(s[g], k), sub(x[g], k)
            if k < 7:
                t = jnp.where(rows > k, c[k] * inv[k], 0.0)
                for k2 in range(k + 1, 8):
                    q[k][k2] = sub(c[k2], k)
                    c[k2] = c[k2] - t * q[k][k2]
                s[g] = s[g] - t * sr[k]
                x[g] = x[g] - t * xr[k]
        for i in range(g + 1, 16):
            ci = [lane(s[i], 8 * g + k) for k in range(8)]
            for k in range(8):
                t = ci[k] * inv[k]
                for k2 in range(k + 1, 8):
                    ci[k2] = ci[k2] - t * q[k][k2]
                s[i] = s[i] - t * sr[k]
                x[i] = x[i] - t * xr[k]
    return jnp.concatenate(s, 0), jnp.concatenate(x, 0)


def factor_tile(w_ref, l_ref, v_ref):
    v_ref[...] = jnp.zeros((TILE, TILE), F32)
    l_ref[...] = jnp.zeros((TILE, TILE), F32)
    rows = lax.broadcasted_iota(jnp.int32, (NB, NB), 0)
    cols = lax.broadcasted_iota(jnp.int32, (NB, NB), 1)

    def step(b, carry):
        off = pl.multiple_of(b * NB, NB)
        sb, xb = block_factor([w_ref[pl.ds(off + 8 * i, 8), pl.ds(off, NB)] for i in range(16)])
        d = jnp.sum(jnp.where(rows == cols, sb, 0.0), axis=1, keepdims=True)
        r = lax.rsqrt(d)
        lb = jnp.where(cols >= rows, sb * r, 0.0).T
        vb = jnp.where(cols <= rows, xb * r, 0.0)
        for bb in range(NBLK):

            @pl.when(b == bb)
            def _(bb=bb):
                o = bb * NB
                e = o + NB
                l_ref[o:e, o:e] = lb
                if bb > 0:
                    v_ref[o:e, :o] = jnp.dot(vb, v_ref[o:e, :o], precision=HIGHEST, preferred_element_type=F32)
                v_ref[o:e, o:e] = vb
                if bb < NBLK - 1:
                    lp = times_t(w_ref[e:, o:e], vb)
                    l_ref[e:, o:e] = lp
                    w_ref[e:, e:] -= times_t(lp, lp)
                    v_ref[e:, :e] -= jnp.dot(lp, v_ref[o:e, :e], precision=HIGHEST, preferred_element_type=F32)

        return carry

    lax.fori_loop(0, NBLK, step, 0)


def assemble(dst_ref, mine_ref, other_ref, t, where_ref):
    y, core = where_ref[0], where_ref[1]
    for m in range(4):
        at = lax.rem(y + 4 - m, 4) * 2
        for src, k in ((mine_ref, core), (other_ref, 1 - core)):
            dst_ref[pl.ds(pl.multiple_of((at + k) * PART, PART), PART), :] = src[m, t]


def first_kernel(where_ref, mine_ref, other_ref, l_ref, v_ref, w_ref):
    assemble(w_ref, mine_ref, other_ref, 0, where_ref)
    factor_tile(w_ref, l_ref, v_ref)


def factor_first(where, mine, other):
    return pl.pallas_call(
        first_kernel,
        out_shape=square(2),
        in_specs=[SMEM, VMEM, VMEM],
        out_specs=(VMEM,) * 2,
        scratch_shapes=[pltpu.VMEM((TILE, TILE), F32)],
        cost_estimate=pl.CostEstimate(flops=10**10, bytes_accessed=3 << 20, transcendentals=0),
        name="factor_first",
    )(where, mine, other)


def second_kernel(where_ref, mine_ref, other_ref, v0_ref, p_ref, l_ref, v_ref, w_ref):
    assemble(w_ref, mine_ref, other_ref, 0, where_ref)
    p_ref[...] = times_t(w_ref[...], v0_ref[...])
    assemble(w_ref, mine_ref, other_ref, 1, where_ref)
    w_ref[...] -= times_t(p_ref[...], p_ref[...])
    factor_tile(w_ref, l_ref, v_ref)


def factor_second(where, mine, other, inverse0):
    return pl.pallas_call(
        second_kernel,
        out_shape=square(3),
        in_specs=[SMEM, VMEM, VMEM, VMEM],
        out_specs=(VMEM,) * 3,
        scratch_shapes=[pltpu.VMEM((TILE, TILE), F32)],
        cost_estimate=pl.CostEstimate(flops=10**10, bytes_accessed=6 << 20, transcendentals=0),
        name="factor_second",
    )(where, mine, other, inverse0)


def split(v):
    hi = v.astype(jnp.bfloat16)
    return hi, (v - hi.astype(F32)).astype(jnp.bfloat16)


def times_t3(a, b):
    def one(p, q):
        return lax.dot_general(p, q, (((1,), (1,)), ((), ())), preferred_element_type=F32)

    return one(a[0], b[0]) + (one(a[0], b[1]) + one(a[1], b[0]))


def prepare_kernel(where_ref, mine_ref, other_ref, v0_ref, p01_ref, v1_ref, p0_ref, p1_ref, w_ref):
    assemble(w_ref, mine_ref, other_ref, 0, where_ref)
    p0 = times_t3(split(w_ref[...]), split(v0_ref[...]))
    p0_ref[...] = p0
    assemble(w_ref, mine_ref, other_ref, 1, where_ref)
    next1 = w_ref[...] - times_t3(split(p0), split(p01_ref[...]))
    p1_ref[...] = times_t3(split(next1), split(v1_ref[...]))


def prepare(where, mine, other, inverse0, p01, inverse1):
    return pl.pallas_call(
        prepare_kernel,
        out_shape=square(2),
        in_specs=[SMEM] + [VMEM] * 5,
        out_specs=(VMEM,) * 2,
        scratch_shapes=[pltpu.VMEM((TILE, TILE), F32)],
        cost_estimate=pl.CostEstimate(flops=3 * 10**9, bytes_accessed=9 << 20, transcendentals=0),
        name="prepare",
    )(where, mine, other, inverse0, p01, inverse1)


UPDATE_BOTH, UPDATE_SECOND, KEEP, PANEL0, PANEL1, LATE_PANEL1, FACTOR0, FACTOR1 = range(8)


def finish_kernel(at_ref, kind_ref, raw_ref, a_ref, v0, p01, v1, p0j, p1j, f0, f1, o_ref, hi_ref, lo_ref):
    s = pl.program_id(0)
    kind = kind_ref[s]

    @pl.when(s == 0)
    def _():
        for n, ref in enumerate((v0, p01, v1, p0j, p1j)):
            hi, lo = split(ref[...])
            hi_ref[n] = hi
            lo_ref[n] = lo

    def times(v, n):
        return times_t3(split(v), (hi_ref[n], lo_ref[n]))

    def rows(h, t):
        return raw_ref[4 * h : 4 * h + 4, t].reshape(TILE // 2, TILE)

    for h in range(2):
        half = pl.ds(h * (TILE // 2), TILE // 2)

        @pl.when(kind == UPDATE_BOTH)
        def _(h=h, half=half):
            p0 = times(rows(h, 0), 0)
            p1 = times(rows(h, 1) - times(p0, 1), 2)
            o_ref[0, half, :] = a_ref[0, half, :] - times(p0, 3) - times(p1, 4)

        @pl.when(kind == UPDATE_SECOND)
        def _(h=h, half=half):
            o_ref[0, half, :] = a_ref[0, half, :] - times(times(rows(h, 1), 2), 4)

        @pl.when(kind == PANEL0)
        def _(h=h, half=half):
            o_ref[0, half, :] = times(rows(h, 0), 0)

        @pl.when(kind == PANEL1)
        def _(h=h, half=half):
            p0 = times(rows(h, 0), 0)
            o_ref[0, half, :] = times(rows(h, 1) - times(p0, 1), 2)

        @pl.when(kind == LATE_PANEL1)
        def _(h=h, half=half):
            o_ref[0, half, :] = times(rows(h, 1), 2)

    @pl.when(kind == KEEP)
    def _():
        o_ref[...] = a_ref[...]

    @pl.when(kind == FACTOR0)
    def _():
        o_ref[0] = f0[...]

    @pl.when(kind == FACTOR1)
    def _():
        o_ref[0] = f1[...]


def finish(at, kind, panels, local, inverse0, p01, inverse1, p0j, p1j, factor0, factor1):
    whole = pl.BlockSpec((TILE, TILE), lambda s, at, kind: (0, 0))
    tile = pl.BlockSpec((1, TILE, TILE), lambda s, at, kind: (s, 0, 0))
    return pl.pallas_call(
        finish_kernel,
        out_shape=jax.ShapeDtypeStruct(local.shape, F32),
        grid_spec=pltpu.PrefetchScalarGridSpec(
            num_scalar_prefetch=2,
            grid=(local.shape[0],),
            in_specs=[pl.BlockSpec((8, 2, PART, TILE), lambda s, at, kind: (at[s], 0, 0, 0)), tile] + [whole] * 7,
            out_specs=tile,
            scratch_shapes=[pltpu.VMEM((5, TILE, TILE), jnp.bfloat16)] * 2,
        ),
        cost_estimate=pl.CostEstimate(flops=3 * 10**10, bytes_accessed=24 << 20, transcendentals=0),
        name="finish",
    )(at, kind, panels, local, inverse0, p01, inverse1, p0j, p1j, factor0, factor1)


BANDT = 32
ROWS = 8
COLS = 32
AX = ("row", "col")


def lin(r, c):
    return (r % ROWS) * COLS + c % COLS


def zx(z, x):
    return (z % 8) * 4 + x % 4


def permute(v, pairs):
    return lax.ppermute(v, AX, [(lin(*a), lin(*b)) for a, b in pairs])


EVERY = [(r, z, x) for r in range(ROWS) for z in range(8) for x in range(4)]


def core_swap(v):
    return permute(v, [((r, zx(z, x)), (r ^ 1, zx(z, x))) for r, z, x in EVERY])


def y_shift(v, k):
    return permute(v, [((r, zx(z, x)), (r + 2 * k, zx(z, x))) for r, z, x in EVERY])


def x_deal(v, k):
    return permute(v, [((r, zx(z, x)), (r, zx(z, x + k))) for r, z, x in EVERY if x < 2])


def z_deal(v, k):
    return permute(v, [((r, zx(0, x)), (r, zx(k, x))) for r, z, x in EVERY if z == 0 and x < 2])


def pick(choices):
    total = None
    for cond, v in choices:
        v = jnp.where(cond, v, 0.0)
        total = v if total is None else total + v
    return total


def spread_x(v, x):
    got = permute(v, [((r, zx(0, 0)), (r, zx(0, 2))) for r in range(ROWS)])
    v = jnp.where(x == 2, got, v)
    got = permute(v, [((r, zx(0, a)), (r, zx(0, a + 1))) for r in range(ROWS) for a in (0, 2)])
    return jnp.where(x % 2 == 1, got, v)


def spread_z(v, z):
    for step in (4, 2, 1):
        pairs = [((r, zx(a, b)), (r, zx(a + step, b))) for r in range(ROWS) for a in range(0, 8, 2 * step) for b in range(4)]
        got = permute(v, pairs)
        v = jnp.where(z % (2 * step) == step, got, v)
    return v


def row_gather(piece):
    mine = jnp.stack([piece] + [y_shift(piece, m) for m in range(1, 4)])
    return mine, core_swap(mine)


def shards(band):
    slots, _, _, _, tile, _ = band.shape
    part = tile // ROWS
    row = lax.axis_index("row")
    col = lax.axis_index("col")
    z, x = col // 4, col % 4
    y, core = row // 2, row % 2
    local = band.reshape(slots, tile, tile)
    where = jnp.stack([y, core]).astype(jnp.int32)

    eighths = local.reshape(8, slots * tile // 8, tile)
    skip = jnp.where((row == 0) & (x == 1), 6, 0)

    def eighth(k):
        return lax.dynamic_index_in_dim(eighths, (skip + k) % 8, 0, keepdims=False)

    arrived = [z_deal(eighth(k), k) for k in range(1, 8)]

    partner = core_swap(local[0])
    even = jnp.where(core == 0, local[0], partner).reshape(4, 2, part, tile)
    odd = jnp.where(core == 0, partner, local[0]).reshape(4, 2, part, tile)
    both = jnp.stack([even, odd], 1)
    both = lax.dynamic_index_in_dim(both, core, 2, keepdims=False)
    mine = [(y == 0, both[0])] + [(y == k, y_shift(both[k], k)) for k in range(1, 4)]
    mine = pick(mine)
    first = spread_x(mine[:1], x)
    beside = permute(mine[1], [((r, 1), (r, 0)) for r in range(ROWS)])
    second = spread_x(jnp.stack([mine[1], beside]), x)
    first, second, arrived = lax.optimization_barrier((first, second, arrived))
    first, second = spread_z(first, z), spread_z(second, z)
    factor0, inverse0 = factor_first(where, *row_gather(first))

    dealt = pick([(z == 0, eighth(0))] + [(z == k, arrived[k - 1]) for k in range(1, 8)])
    fourths = dealt.reshape(4, part, tile)
    p0, p1 = [(x == 0, fourths[0])], [(x == 1, fourths[1])]
    for k in range(1, 4):
        got = x_deal(jnp.where(x == 0, fourths[k], fourths[(k + 1) % 4]), k)
        p0.append((x == k, got))
        p1.append((x == (k + 1) % 4, got))
    piece = jnp.stack([pick(p0), pick(p1)])
    panels = lax.all_gather(piece, "col")

    pairs = [((r, 8 * s + q), (q, 8 * s + r)) for s in range(slots) for r in range(ROWS) for q in range(ROWS)]
    crossed = row_gather(permute(piece, pairs))

    p01, factor1, inverse1 = factor_second(where, *row_gather(second), inverse0)
    p0j, p1j = prepare(where, *crossed, inverse0, p01, inverse1)

    rows_here = col + (row - col) % ROWS + ROWS * jnp.arange(slots, dtype=jnp.int32)
    at = (rows_here // ROWS) % slots
    update = jnp.where(rows_here < BANDT, UPDATE_BOTH, jnp.where(rows_here == BANDT, UPDATE_SECOND, KEEP))
    panel0 = jnp.where(rows_here == 0, FACTOR0, PANEL0)
    panel1 = jnp.where(rows_here == 1, FACTOR1, jnp.where(rows_here == BANDT, LATE_PANEL1, PANEL1))
    kind = jnp.where(col == 0, panel0, jnp.where(col == 1, panel1, update)).astype(jnp.int32)
    out = finish(at, kind, panels, local, inverse0, p01, inverse1, p0j, p1j, factor0, factor1)
    return out.reshape(band.shape)


def solution(mesh):
    spec = P(None, "row", None, "col", None, None)
    return jax.shard_map(shards, mesh=mesh, in_specs=(spec,), out_specs=spec, check_vma=False)
```

```python
import jax
import jax.numpy as jnp
from jax import lax
from jax.experimental import pallas as pl
from jax.experimental.pallas import tpu as pltpu
from jax.sharding import PartitionSpec as P


TILE = 512
NB = 128
NBLK = TILE // NB
PART = TILE // 8
HIGHEST = lax.Precision.HIGHEST
VMEM = pl.BlockSpec(memory_space=pltpu.VMEM)
SMEM = pl.BlockSpec(memory_space=pltpu.SMEM)
F32 = jnp.float32


def square(n=1):
    return (jax.ShapeDtypeStruct((TILE, TILE), F32),) * n


def times_t(a, b):
    return lax.dot_general(a, b, (((1,), (1,)), ((), ())), precision=HIGHEST, preferred_element_type=F32)


def block_factor(s):
    rows = lax.broadcasted_iota(jnp.int32, (8, NB), 0)
    cols = lax.broadcasted_iota(jnp.int32, (8, NB), 1)
    x = [jnp.where(cols == rows + 8 * i, 1.0, 0.0).astype(F32) for i in range(16)]

    def lane(v, c):
        return jnp.broadcast_to(v[:, c : c + 1], (8, NB))

    def sub(v, j):
        return jnp.broadcast_to(v[j : j + 1, :], (8, NB))

    for g in range(16):
        c = [lane(s[g], 8 * g + k) for k in range(8)]
        inv, q, sr, xr = [None] * 8, [[None] * 8 for _ in range(8)], [None] * 8, [None] * 8
        for k in range(8):
            inv[k] = 1.0 / sub(c[k], k)
            sr[k], xr[k] = sub(s[g], k), sub(x[g], k)
            if k < 7:
                t = jnp.where(rows > k, c[k] * inv[k], 0.0)
                for k2 in range(k + 1, 8):
                    q[k][k2] = sub(c[k2], k)
                    c[k2] = c[k2] - t * q[k][k2]
                s[g] = s[g] - t * sr[k]
                x[g] = x[g] - t * xr[k]
        for i in range(g + 1, 16):
            ci = [lane(s[i], 8 * g + k) for k in range(8)]
            for k in range(8):
                t = ci[k] * inv[k]
                for k2 in range(k + 1, 8):
                    ci[k2] = ci[k2] - t * q[k][k2]
                s[i] = s[i] - t * sr[k]
                x[i] = x[i] - t * xr[k]
    return jnp.concatenate(s, 0), jnp.concatenate(x, 0)


def factor_tile(w_ref, l_ref, v_ref):
    v_ref[...] = jnp.zeros((TILE, TILE), F32)
    l_ref[...] = jnp.zeros((TILE, TILE), F32)
    rows = lax.broadcasted_iota(jnp.int32, (NB, NB), 0)
    cols = lax.broadcasted_iota(jnp.int32, (NB, NB), 1)

    def step(b, carry):
        off = pl.multiple_of(b * NB, NB)
        sb, xb = block_factor([w_ref[pl.ds(off + 8 * i, 8), pl.ds(off, NB)] for i in range(16)])
        d = jnp.sum(jnp.where(rows == cols, sb, 0.0), axis=1, keepdims=True)
        r = lax.rsqrt(d)
        lb = jnp.where(cols >= rows, sb * r, 0.0).T
        vb = jnp.where(cols <= rows, xb * r, 0.0)
        for bb in range(NBLK):

            @pl.when(b == bb)
            def _(bb=bb):
                o = bb * NB
                e = o + NB
                l_ref[o:e, o:e] = lb
                if bb > 0:
                    v_ref[o:e, :o] = jnp.dot(vb, v_ref[o:e, :o], precision=HIGHEST, preferred_element_type=F32)
                v_ref[o:e, o:e] = vb
                if bb < NBLK - 1:
                    lp = times_t(w_ref[e:, o:e], vb)
                    l_ref[e:, o:e] = lp
                    w_ref[e:, e:] -= times_t(lp, lp)
                    v_ref[e:, :e] -= jnp.dot(lp, v_ref[o:e, :e], precision=HIGHEST, preferred_element_type=F32)

        return carry

    lax.fori_loop(0, NBLK, step, 0)


def assemble(dst_ref, mine_ref, other_ref, t, where_ref):
    y, core = where_ref[0], where_ref[1]
    for m in range(4):
        at = lax.rem(y + 4 - m, 4) * 2
        for src, k in ((mine_ref, core), (other_ref, 1 - core)):
            dst_ref[pl.ds(pl.multiple_of((at + k) * PART, PART), PART), :] = src[m, t]


def first_kernel(where_ref, mine_ref, other_ref, l_ref, v_ref, w_ref):
    assemble(w_ref, mine_ref, other_ref, 0, where_ref)
    factor_tile(w_ref, l_ref, v_ref)


def factor_first(where, mine, other):
    return pl.pallas_call(
        first_kernel,
        out_shape=square(2),
        in_specs=[SMEM, VMEM, VMEM],
        out_specs=(VMEM,) * 2,
        scratch_shapes=[pltpu.VMEM((TILE, TILE), F32)],
        cost_estimate=pl.CostEstimate(flops=10**10, bytes_accessed=3 << 20, transcendentals=0),
        name="factor_first",
    )(where, mine, other)


def second_kernel(where_ref, mine_ref, other_ref, v0_ref, p_ref, l_ref, v_ref, w_ref):
    assemble(w_ref, mine_ref, other_ref, 0, where_ref)
    p_ref[...] = times_t(w_ref[...], v0_ref[...])
    assemble(w_ref, mine_ref, other_ref, 1, where_ref)
    w_ref[...] -= times_t(p_ref[...], p_ref[...])
    factor_tile(w_ref, l_ref, v_ref)


def factor_second(where, mine, other, inverse0):
    return pl.pallas_call(
        second_kernel,
        out_shape=square(3),
        in_specs=[SMEM, VMEM, VMEM, VMEM],
        out_specs=(VMEM,) * 3,
        scratch_shapes=[pltpu.VMEM((TILE, TILE), F32)],
        cost_estimate=pl.CostEstimate(flops=10**10, bytes_accessed=6 << 20, transcendentals=0),
        name="factor_second",
    )(where, mine, other, inverse0)


def split(v):
    hi = v.astype(jnp.bfloat16)
    return hi, (v - hi.astype(F32)).astype(jnp.bfloat16)


def times_t3(a, b):
    def one(p, q):
        return lax.dot_general(p, q, (((1,), (1,)), ((), ())), preferred_element_type=F32)

    return one(a[0], b[0]) + (one(a[0], b[1]) + one(a[1], b[0]))


def prepare_kernel(where_ref, mine_ref, other_ref, v0_ref, p01_ref, v1_ref, p0_ref, p1_ref, w_ref):
    assemble(w_ref, mine_ref, other_ref, 0, where_ref)
    p0 = times_t3(split(w_ref[...]), split(v0_ref[...]))
    p0_ref[...] = p0
    assemble(w_ref, mine_ref, other_ref, 1, where_ref)
    next1 = w_ref[...] - times_t3(split(p0), split(p01_ref[...]))
    p1_ref[...] = times_t3(split(next1), split(v1_ref[...]))


def prepare(where, mine, other, inverse0, p01, inverse1):
    return pl.pallas_call(
        prepare_kernel,
        out_shape=square(2),
        in_specs=[SMEM] + [VMEM] * 5,
        out_specs=(VMEM,) * 2,
        scratch_shapes=[pltpu.VMEM((TILE, TILE), F32)],
        cost_estimate=pl.CostEstimate(flops=3 * 10**9, bytes_accessed=9 << 20, transcendentals=0),
        name="prepare",
    )(where, mine, other, inverse0, p01, inverse1)


UPDATE_BOTH, UPDATE_SECOND, KEEP, PANEL0, PANEL1, LATE_PANEL1, FACTOR0, FACTOR1 = range(8)


HALF = TILE // 2


def finish_kernel(at_ref, kind_ref, raw_ref, a_ref, v0, p01, v1, p0j, p1j, f0, f1, o_ref, w_ref):
    kind = kind_ref[pl.program_id(0)]

    @pl.when((pl.program_id(0) == 0) & (pl.program_id(1) == 0))
    def _():
        for n, ref in enumerate((v0, p01, v1, p0j, p1j)):
            hi, lo = split(ref[...])
            w_ref[n] = jnp.concatenate([hi, lo, hi], 1)

    def times(v, n):
        hi, lo = split(v)
        return lax.dot_general(
            jnp.concatenate([hi, hi, lo], 1), w_ref[n], (((1,), (1,)), ((), ())), preferred_element_type=F32
        )

    def raw(t):
        return raw_ref[:, t].reshape(HALF, TILE)

    @pl.when(kind == UPDATE_BOTH)
    def _():
        p0 = times(raw(0), 0)
        p1 = times(raw(1) - times(p0, 1), 2)
        o_ref[0] = a_ref[0] - times(p0, 3) - times(p1, 4)

    @pl.when(kind == UPDATE_SECOND)
    def _():
        o_ref[0] = a_ref[0] - times(times(raw(1), 2), 4)

    @pl.when(kind == PANEL0)
    def _():
        o_ref[0] = times(raw(0), 0)

    @pl.when(kind == PANEL1)
    def _():
        p0 = times(raw(0), 0)
        o_ref[0] = times(raw(1) - times(p0, 1), 2)

    @pl.when(kind == LATE_PANEL1)
    def _():
        o_ref[0] = times(raw(1), 2)

    @pl.when(kind == KEEP)
    def _():
        o_ref[...] = a_ref[...]

    @pl.when(kind == FACTOR0)
    def _():
        o_ref[0] = f0[...]

    @pl.when(kind == FACTOR1)
    def _():
        o_ref[0] = f1[...]


def finish(at, kind, panels, local, inverse0, p01, inverse1, p0j, p1j, factor0, factor1):
    whole = pl.BlockSpec((TILE, TILE), lambda s, h, at, kind: (0, 0))
    tile = pl.BlockSpec((1, HALF, TILE), lambda s, h, at, kind: (s, h, 0))
    half = pl.BlockSpec((HALF, TILE), lambda s, h, at, kind: (h, 0))
    return pl.pallas_call(
        finish_kernel,
        out_shape=jax.ShapeDtypeStruct(local.shape, F32),
        grid_spec=pltpu.PrefetchScalarGridSpec(
            num_scalar_prefetch=2,
            grid=(local.shape[0], 2),
            in_specs=[pl.BlockSpec((4, 2, PART, TILE), lambda s, h, at, kind: (2 * at[s] + h, 0, 0, 0)), tile]
            + [whole] * 5
            + [half] * 2,
            out_specs=tile,
            scratch_shapes=[pltpu.VMEM((5, TILE, 3 * TILE), jnp.bfloat16)],
        ),
        cost_estimate=pl.CostEstimate(flops=3 * 10**10, bytes_accessed=24 << 20, transcendentals=0),
        name="finish",
    )(at, kind, panels, local, inverse0, p01, inverse1, p0j, p1j, factor0, factor1)


BANDT = 32
ROWS = 8
COLS = 32
AX = ("row", "col")


def lin(r, c):
    return (r % ROWS) * COLS + c % COLS


def zx(z, x):
    return (z % 8) * 4 + x % 4


def permute(v, pairs):
    return lax.ppermute(v, AX, [(lin(*a), lin(*b)) for a, b in pairs])


EVERY = [(r, z, x) for r in range(ROWS) for z in range(8) for x in range(4)]


def core_swap(v):
    return permute(v, [((r, zx(z, x)), (r ^ 1, zx(z, x))) for r, z, x in EVERY])


def y_shift(v, k):
    return permute(v, [((r, zx(z, x)), (r + 2 * k, zx(z, x))) for r, z, x in EVERY])


def x_deal(v, k):
    return permute(v, [((r, zx(z, x)), (r, zx(z, x + k))) for r, z, x in EVERY if x < 2])


def z_deal(v, k):
    return permute(v, [((r, zx(0, x)), (r, zx(k, x))) for r, z, x in EVERY if z == 0 and x < 2])


def pick(choices):
    total = None
    for cond, v in choices:
        v = jnp.where(cond, v, 0.0)
        total = v if total is None else total + v
    return total


def spread_x(v, x):
    got = permute(v, [((r, zx(0, 0)), (r, zx(0, 2))) for r in range(ROWS)])
    v = jnp.where(x == 2, got, v)
    got = permute(v, [((r, zx(0, a)), (r, zx(0, a + 1))) for r in range(ROWS) for a in (0, 2)])
    return jnp.where(x % 2 == 1, got, v)


def spread_z(v, z):
    for step in (4, 2, 1):
        pairs = [((r, zx(a, b)), (r, zx(a + step, b))) for r in range(ROWS) for a in range(0, 8, 2 * step) for b in range(4)]
        got = permute(v, pairs)
        v = jnp.where(z % (2 * step) == step, got, v)
    return v


def ring(piece):
    return [piece] + [y_shift(piece, m) for m in range(1, 4)]


def with_partner(pieces):
    mine = jnp.stack(pieces)
    return mine, core_swap(mine)


def shards(band):
    slots, _, _, _, tile, _ = band.shape
    part = tile // ROWS
    row = lax.axis_index("row")
    col = lax.axis_index("col")
    z, x = col // 4, col % 4
    y, core = row // 2, row % 2
    local = band.reshape(slots, tile, tile)
    where = jnp.stack([y, core]).astype(jnp.int32)

    eighths = local.reshape(8, slots * tile // 8, tile)
    skip = jnp.where((row == 0) & (x == 1), 6, 0)

    def eighth(k):
        return lax.dynamic_index_in_dim(eighths, (skip + k) % 8, 0, keepdims=False)

    arrived = [z_deal(eighth(k), k) for k in range(1, 8)]

    partner = core_swap(local[0])
    even = jnp.where(core == 0, local[0], partner).reshape(4, 2, part, tile)
    odd = jnp.where(core == 0, partner, local[0]).reshape(4, 2, part, tile)
    both = jnp.stack([even, odd], 1)
    both = lax.dynamic_index_in_dim(both, core, 2, keepdims=False)
    mine = [(y == 0, both[0])] + [(y == k, y_shift(both[k], k)) for k in range(1, 4)]
    mine = pick(mine)
    first = spread_x(mine[:1], x)
    beside = permute(mine[1], [((r, 1), (r, 0)) for r in range(ROWS)])
    second = spread_x(jnp.stack([mine[1], beside]), x)
    first, second, arrived = lax.optimization_barrier((first, second, arrived))
    first, second = spread_z(first, z), spread_z(second, z)
    first, second = with_partner(ring(first)), ring(second)

    dealt = pick([(z == 0, eighth(0))] + [(z == k, arrived[k - 1]) for k in range(1, 8)])
    fourths = dealt.reshape(4, part, tile)
    p0, p1 = [(x == 0, fourths[0])], [(x == 1, fourths[1])]
    for k in range(1, 4):
        got = x_deal(jnp.where(x == 0, fourths[k], fourths[(k + 1) % 4]), k)
        p0.append((x == k, got))
        p1.append((x == (k + 1) % 4, got))
    piece = jnp.stack([pick(p0), pick(p1)])
    panels = lax.all_gather(piece, "col")

    pairs = [((r, 8 * s + q), (q, 8 * s + r)) for s in range(slots) for r in range(ROWS) for q in range(ROWS)]
    crossed = ring(permute(piece, pairs))
    factor0, inverse0 = factor_first(where, *first)
    inverse0, second, crossed = lax.optimization_barrier((inverse0, second, crossed))
    second, crossed = with_partner(second), with_partner(crossed)

    p01, factor1, inverse1 = factor_second(where, *second, inverse0)
    p0j, p1j = prepare(where, *crossed, inverse0, p01, inverse1)

    rows_here = col + (row - col) % ROWS + ROWS * jnp.arange(slots, dtype=jnp.int32)
    at = (rows_here // ROWS) % slots
    update = jnp.where(rows_here < BANDT, UPDATE_BOTH, jnp.where(rows_here == BANDT, UPDATE_SECOND, KEEP))
    panel0 = jnp.where(rows_here == 0, FACTOR0, PANEL0)
    panel1 = jnp.where(rows_here == 1, FACTOR1, jnp.where(rows_here == BANDT, LATE_PANEL1, PANEL1))
    kind = jnp.where(col == 0, panel0, jnp.where(col == 1, panel1, update)).astype(jnp.int32)
    out = finish(at, kind, panels, local, inverse0, p01, inverse1, p0j, p1j, factor0, factor1)
    return out.reshape(band.shape)


def solution(mesh):
    spec = P(None, "row", None, "col", None, None)

    return jax.shard_map(shards, mesh=mesh, in_specs=(spec,), out_specs=spec, check_vma=False)
```

```python
import jax
import jax.numpy as jnp
from jax import lax
from jax.experimental import pallas as pl
from jax.experimental.pallas import tpu as pltpu
from jax.sharding import PartitionSpec as P


TILE = 512
NB = 128
NBLK = TILE // NB
PART = TILE // 8
HIGHEST = lax.Precision.HIGHEST
VMEM = pl.BlockSpec(memory_space=pltpu.VMEM)
SMEM = pl.BlockSpec(memory_space=pltpu.SMEM)
F32 = jnp.float32


def square(n=1):
    return (jax.ShapeDtypeStruct((TILE, TILE), F32),) * n


def times_t(a, b):
    return lax.dot_general(a, b, (((1,), (1,)), ((), ())), precision=HIGHEST, preferred_element_type=F32)


def block_factor(s):
    rows = lax.broadcasted_iota(jnp.int32, (8, NB), 0)
    cols = lax.broadcasted_iota(jnp.int32, (8, NB), 1)

    def lane(v, c):
        return jnp.broadcast_to(v[:, c : c + 1], (8, NB))

    def sub(v, j):
        return jnp.broadcast_to(v[j : j + 1, :], (8, NB))

    upper, inverse = [None] * 16, [None] * 16
    for g in range(16):
        o = 8 * g
        inside = (cols >= o) & (cols < o + 8)
        c = [lane(s[g], o + k) for k in range(8)]
        s[g] = jnp.where(inside, jnp.where(cols == rows + o, 1.0, 0.0), s[g])
        inv, q, sr = [None] * 8, [[None] * 8 for _ in range(8)], [None] * 8
        pivots = None
        for k in range(8):
            piv = sub(c[k], k)
            pivots = piv if k == 0 else jnp.where(rows == k, piv, pivots)
            inv[k] = 1.0 / piv
            sr[k] = sub(s[g], k)
            if k < 7:
                t = jnp.where(rows > k, c[k] * inv[k], 0.0)
                for k2 in range(k + 1, 8):
                    q[k][k2] = sub(c[k2], k)
                    c[k2] = c[k2] - t * q[k][k2]
                s[g] = s[g] - t * sr[k]
        for i in range(g + 1, 16):
            ci = [lane(s[i], o + k) for k in range(8)]
            s[i] = jnp.where(inside, 0.0, s[i])
            for k in range(8):
                t = ci[k] * inv[k]
                for k2 in range(k + 1, 8):
                    ci[k2] = ci[k2] - t * q[k][k2]
                s[i] = s[i] - t * sr[k]
        block = s[g]
        for k in range(8):
            block = jnp.where(cols == o + k, c[k], block)
        r = lax.rsqrt(pivots)
        upper[g] = jnp.where(cols >= rows + o, block * r, 0.0)
        inverse[g] = jnp.where(cols <= rows + o, s[g] * r, 0.0)
    return jnp.concatenate(upper, 0), jnp.concatenate(inverse, 0)


def factor_tile(w_ref, l_ref, v_ref):
    v_ref[...] = jnp.zeros((TILE, TILE), F32)
    l_ref[...] = jnp.zeros((TILE, TILE), F32)

    def step(b, carry):
        off = pl.multiple_of(b * NB, NB)
        ub, vb = block_factor([w_ref[pl.ds(off + 8 * i, 8), pl.ds(off, NB)] for i in range(16)])
        lb = ub.T
        for bb in range(NBLK):

            @pl.when(b == bb)
            def _(bb=bb):
                o = bb * NB
                e = o + NB
                l_ref[o:e, o:e] = lb
                if bb > 0:
                    v_ref[o:e, :o] = jnp.dot(vb, v_ref[o:e, :o], precision=HIGHEST, preferred_element_type=F32)
                v_ref[o:e, o:e] = vb
                if bb < NBLK - 1:
                    lp = times_t(w_ref[e:, o:e], vb)
                    l_ref[e:, o:e] = lp
                    w_ref[e:, e:] -= times_t(lp, lp)
                    v_ref[e:, :e] -= jnp.dot(lp, v_ref[o:e, :e], precision=HIGHEST, preferred_element_type=F32)

        return carry

    lax.fori_loop(0, NBLK, step, 0)


def assemble(dst_ref, mine_ref, other_ref, t, where_ref):
    y, core = where_ref[0], where_ref[1]
    for m in range(4):
        at = lax.rem(y + 4 - m, 4) * 2
        for src, k in ((mine_ref, core), (other_ref, 1 - core)):
            dst_ref[pl.ds(pl.multiple_of((at + k) * PART, PART), PART), :] = src[m, t]


def first_kernel(where_ref, mine_ref, other_ref, l_ref, v_ref, w_ref):
    assemble(w_ref, mine_ref, other_ref, 0, where_ref)
    factor_tile(w_ref, l_ref, v_ref)


def factor_first(where, mine, other):
    return pl.pallas_call(
        first_kernel,
        out_shape=square(2),
        in_specs=[SMEM, VMEM, VMEM],
        out_specs=(VMEM,) * 2,
        scratch_shapes=[pltpu.VMEM((TILE, TILE), F32)],
        cost_estimate=pl.CostEstimate(flops=10**10, bytes_accessed=3 << 20, transcendentals=0),
        name="factor_first",
    )(where, mine, other)


def second_kernel(where_ref, mine_ref, other_ref, v0_ref, p_ref, l_ref, v_ref, w_ref):
    assemble(w_ref, mine_ref, other_ref, 0, where_ref)
    p_ref[...] = times_t(w_ref[...], v0_ref[...])
    assemble(w_ref, mine_ref, other_ref, 1, where_ref)
    w_ref[...] -= times_t(p_ref[...], p_ref[...])
    factor_tile(w_ref, l_ref, v_ref)


def factor_second(where, mine, other, inverse0):
    return pl.pallas_call(
        second_kernel,
        out_shape=square(3),
        in_specs=[SMEM, VMEM, VMEM, VMEM],
        out_specs=(VMEM,) * 3,
        scratch_shapes=[pltpu.VMEM((TILE, TILE), F32)],
        cost_estimate=pl.CostEstimate(flops=10**10, bytes_accessed=6 << 20, transcendentals=0),
        name="factor_second",
    )(where, mine, other, inverse0)


def split(v):
    hi = v.astype(jnp.bfloat16)
    return hi, (v - hi.astype(F32)).astype(jnp.bfloat16)


def times_t3(a, b):
    def one(p, q):
        return lax.dot_general(p, q, (((1,), (1,)), ((), ())), preferred_element_type=F32)

    return one(a[0], b[0]) + (one(a[0], b[1]) + one(a[1], b[0]))


def prepare_kernel(where_ref, mine_ref, other_ref, v0_ref, p01_ref, v1_ref, p0_ref, p1_ref, w_ref):
    assemble(w_ref, mine_ref, other_ref, 2, where_ref)
    p0 = times_t3(split(w_ref[...]), split(v0_ref[...]))
    p0_ref[...] = p0
    assemble(w_ref, mine_ref, other_ref, 3, where_ref)
    next1 = w_ref[...] - times_t3(split(p0), split(p01_ref[...]))
    p1_ref[...] = times_t3(split(next1), split(v1_ref[...]))


def prepare(where, mine, other, inverse0, p01, inverse1):
    return pl.pallas_call(
        prepare_kernel,
        out_shape=square(2),
        in_specs=[SMEM] + [VMEM] * 5,
        out_specs=(VMEM,) * 2,
        scratch_shapes=[pltpu.VMEM((TILE, TILE), F32)],
        cost_estimate=pl.CostEstimate(flops=3 * 10**9, bytes_accessed=9 << 20, transcendentals=0),
        name="prepare",
    )(where, mine, other, inverse0, p01, inverse1)


UPDATE_BOTH, UPDATE_SECOND, KEEP, PANEL0, PANEL1, LATE_PANEL1, FACTOR0, FACTOR1 = range(8)


HALF = TILE // 2


def finish_kernel(at_ref, kind_ref, raw_ref, a_ref, v0, p01, v1, p0j, p1j, f0, f1, o_ref, w_ref):
    kind = kind_ref[pl.program_id(0)]

    @pl.when((pl.program_id(0) == 0) & (pl.program_id(1) == 0))
    def _():
        for n, ref in enumerate((v0, p01, v1, p0j, p1j)):
            hi, lo = split(ref[...])
            w_ref[n] = jnp.concatenate([hi, lo, hi], 1)

    def times(v, n):
        hi, lo = split(v)
        return lax.dot_general(
            jnp.concatenate([hi, hi, lo], 1), w_ref[n], (((1,), (1,)), ((), ())), preferred_element_type=F32
        )

    def raw(t):
        return raw_ref[:, t].reshape(HALF, TILE)

    @pl.when(kind == UPDATE_BOTH)
    def _():
        p0 = times(raw(0), 0)
        p1 = times(raw(1) - times(p0, 1), 2)
        o_ref[0] = a_ref[0] - times(p0, 3) - times(p1, 4)

    @pl.when(kind == UPDATE_SECOND)
    def _():
        o_ref[0] = a_ref[0] - times(times(raw(1), 2), 4)

    @pl.when(kind == PANEL0)
    def _():
        o_ref[0] = times(raw(0), 0)

    @pl.when(kind == PANEL1)
    def _():
        p0 = times(raw(0), 0)
        o_ref[0] = times(raw(1) - times(p0, 1), 2)

    @pl.when(kind == LATE_PANEL1)
    def _():
        o_ref[0] = times(raw(1), 2)

    @pl.when(kind == KEEP)
    def _():
        o_ref[...] = a_ref[...]

    @pl.when(kind == FACTOR0)
    def _():
        o_ref[0] = f0[...]

    @pl.when(kind == FACTOR1)
    def _():
        o_ref[0] = f1[...]


def finish(at, kind, panels, local, inverse0, p01, inverse1, p0j, p1j, factor0, factor1):
    whole = pl.BlockSpec((TILE, TILE), lambda s, h, at, kind: (0, 0))
    tile = pl.BlockSpec((1, HALF, TILE), lambda s, h, at, kind: (s, h, 0))
    half = pl.BlockSpec((HALF, TILE), lambda s, h, at, kind: (h, 0))
    return pl.pallas_call(
        finish_kernel,
        out_shape=jax.ShapeDtypeStruct(local.shape, F32),
        grid_spec=pltpu.PrefetchScalarGridSpec(
            num_scalar_prefetch=2,
            grid=(local.shape[0], 2),
            in_specs=[pl.BlockSpec((4, 2, PART, TILE), lambda s, h, at, kind: (2 * at[s] + h, 0, 0, 0)), tile]
            + [whole] * 5
            + [half] * 2,
            out_specs=tile,
            scratch_shapes=[pltpu.VMEM((5, TILE, 3 * TILE), jnp.bfloat16)],
        ),
        cost_estimate=pl.CostEstimate(flops=3 * 10**10, bytes_accessed=24 << 20, transcendentals=0),
        name="finish",
    )(at, kind, panels, local, inverse0, p01, inverse1, p0j, p1j, factor0, factor1)


BANDT = 32
ROWS = 8
COLS = 32
AX = ("row", "col")


def lin(r, c):
    return (r % ROWS) * COLS + c % COLS


def zx(z, x):
    return (z % 8) * 4 + x % 4


def permute(v, pairs):
    return lax.ppermute(v, AX, [(lin(*a), lin(*b)) for a, b in pairs])


EVERY = [(r, z, x) for r in range(ROWS) for z in range(8) for x in range(4)]


def core_swap(v):
    return permute(v, [((r, zx(z, x)), (r ^ 1, zx(z, x))) for r, z, x in EVERY])


def y_shift(v, k):
    return permute(v, [((r, zx(z, x)), (r + 2 * k, zx(z, x))) for r, z, x in EVERY])


def x_deal(v, k):
    return permute(v, [((r, zx(z, x)), (r, zx(z, x + k))) for r, z, x in EVERY if x < 2])


def z_deal(v, k):
    return permute(v, [((r, zx(0, x)), (r, zx(k, x))) for r, z, x in EVERY if z == 0 and x < 2])


def pick(choices):
    total = None
    for cond, v in choices:
        v = jnp.where(cond, v, 0.0)
        total = v if total is None else total + v
    return total


def spread_x(v, x):
    got = permute(v, [((r, zx(0, 0)), (r, zx(0, 2))) for r in range(ROWS)])
    v = jnp.where(x == 2, got, v)
    got = permute(v, [((r, zx(0, a)), (r, zx(0, a + 1))) for r in range(ROWS) for a in (0, 2)])
    return jnp.where(x % 2 == 1, got, v)


def spread_z(v, z, steps):
    for step in steps:
        pairs = [((r, zx(a, b)), (r, zx(a + step, b))) for r in range(ROWS) for a in range(0, 8, 2 * step) for b in range(4)]
        got = permute(v, pairs)
        v = jnp.where(z % (2 * step) == step, got, v)
    return v


def ring(piece):
    return [piece] + [y_shift(piece, m) for m in range(1, 4)]


def with_partner(pieces):
    mine = jnp.stack(pieces)
    return mine, core_swap(mine)


def shards(band):
    slots, _, _, _, tile, _ = band.shape
    part = tile // ROWS
    row = lax.axis_index("row")
    col = lax.axis_index("col")
    z, x = col // 4, col % 4
    y, core = row // 2, row % 2
    local = band.reshape(slots, tile, tile)
    where = jnp.stack([y, core]).astype(jnp.int32)

    eighths = local.reshape(8, slots * tile // 8, tile)
    skip = jnp.where((row == 0) & (x == 1), 6, 0)

    def eighth(k):
        return lax.dynamic_index_in_dim(eighths, (skip + k) % 8, 0, keepdims=False)

    arrived = [z_deal(eighth(k), k) for k in range(1, 8)]

    partner = core_swap(local[0])
    even = jnp.where(core == 0, local[0], partner).reshape(4, 2, part, tile)
    odd = jnp.where(core == 0, partner, local[0]).reshape(4, 2, part, tile)
    both = jnp.stack([even, odd], 1)
    both = lax.dynamic_index_in_dim(both, core, 2, keepdims=False)
    mine = [(y == 0, both[0])] + [(y == k, y_shift(both[k], k)) for k in range(1, 4)]
    mine = pick(mine)
    first = spread_z(spread_x(mine[:1], x), z, (4,))
    beside = permute(mine[1], [((r, 1), (r, 0)) for r in range(ROWS)])
    second = spread_x(jnp.stack([mine[1], beside]), x)
    first, second, arrived = lax.optimization_barrier((first, second, arrived))
    first, second = spread_z(first, z, (2, 1)), spread_z(second, z, (4, 2, 1))
    first = with_partner(ring(first))

    dealt = pick([(z == 0, eighth(0))] + [(z == k, arrived[k - 1]) for k in range(1, 8)])
    fourths = dealt.reshape(4, part, tile)
    p0, p1 = [(x == 0, fourths[0])], [(x == 1, fourths[1])]
    for k in range(1, 4):
        got = x_deal(jnp.where(x == 0, fourths[k], fourths[(k + 1) % 4]), k)
        p0.append((x == k, got))
        p1.append((x == (k + 1) % 4, got))
    piece = jnp.stack([pick(p0), pick(p1)])
    panels = lax.all_gather(piece, "col")

    pairs = [((r, 8 * s + q), (q, 8 * s + r)) for s in range(slots) for r in range(ROWS) for q in range(ROWS)]
    rest = ring(jnp.concatenate([second, permute(piece, pairs)]))
    factor0, inverse0 = factor_first(where, *first)
    inverse0, rest = lax.optimization_barrier((inverse0, rest))
    rest = with_partner(rest)
    p01, factor1, inverse1 = factor_second(where, *rest, inverse0)
    p0j, p1j = prepare(where, *rest, inverse0, p01, inverse1)

    rows_here = col + (row - col) % ROWS + ROWS * jnp.arange(slots, dtype=jnp.int32)
    at = (rows_here // ROWS) % slots
    update = jnp.where(rows_here < BANDT, UPDATE_BOTH, jnp.where(rows_here == BANDT, UPDATE_SECOND, KEEP))
    panel0 = jnp.where(rows_here == 0, FACTOR0, PANEL0)
    panel1 = jnp.where(rows_here == 1, FACTOR1, jnp.where(rows_here == BANDT, LATE_PANEL1, PANEL1))
    kind = jnp.where(col == 0, panel0, jnp.where(col == 1, panel1, update)).astype(jnp.int32)
    out = finish(at, kind, panels, local, inverse0, p01, inverse1, p0j, p1j, factor0, factor1)
    return out.reshape(band.shape)


def solution(mesh):
    spec = P(None, "row", None, "col", None, None)

    return jax.shard_map(shards, mesh=mesh, in_specs=(spec,), out_specs=spec, check_vma=False)
```

```python
import jax
import jax.numpy as jnp
from jax import lax
from jax.experimental import pallas as pl
from jax.experimental.pallas import tpu as pltpu
from jax.sharding import PartitionSpec as P


TILE = 512
NB = 128
NBLK = TILE // NB
PART = TILE // 8
HIGHEST = lax.Precision.HIGHEST
VMEM = pl.BlockSpec(memory_space=pltpu.VMEM)
SMEM = pl.BlockSpec(memory_space=pltpu.SMEM)
F32 = jnp.float32


def square(n=1):
    return (jax.ShapeDtypeStruct((TILE, TILE), F32),) * n


def times_t(a, b):
    return lax.dot_general(a, b, (((1,), (1,)), ((), ())), precision=HIGHEST, preferred_element_type=F32)


def block_factor(s):
    rows = lax.broadcasted_iota(jnp.int32, (8, NB), 0)
    cols = lax.broadcasted_iota(jnp.int32, (8, NB), 1)

    def lane(v, c):
        return jnp.broadcast_to(v[:, c : c + 1], (8, NB))

    def sub(v, j):
        return jnp.broadcast_to(v[j : j + 1, :], (8, NB))

    upper, inverse = [None] * 16, [None] * 16
    for g in range(16):
        o = 8 * g
        inside = (cols >= o) & (cols < o + 8)
        c = [lane(s[g], o + k) for k in range(8)]
        s[g] = jnp.where(inside, jnp.where(cols == rows + o, 1.0, 0.0), s[g])
        inv, q, sr = [None] * 8, [[None] * 8 for _ in range(8)], [None] * 8
        pivots = None
        for k in range(8):
            piv = sub(c[k], k)
            pivots = piv if k == 0 else jnp.where(rows == k, piv, pivots)
            inv[k] = 1.0 / piv
            sr[k] = sub(s[g], k)
            if k < 7:
                t = jnp.where(rows > k, c[k] * inv[k], 0.0)
                for k2 in range(k + 1, 8):
                    q[k][k2] = sub(c[k2], k)
                    c[k2] = c[k2] - t * q[k][k2]
                s[g] = s[g] - t * sr[k]
        for i in range(g + 1, 16):
            ci = [lane(s[i], o + k) for k in range(8)]
            s[i] = jnp.where(inside, 0.0, s[i])
            for k in range(8):
                t = ci[k] * inv[k]
                for k2 in range(k + 1, 8):
                    ci[k2] = ci[k2] - t * q[k][k2]
                s[i] = s[i] - t * sr[k]
        block = s[g]
        for k in range(8):
            block = jnp.where(cols == o + k, c[k], block)
        r = lax.rsqrt(pivots)
        upper[g] = jnp.where(cols >= rows + o, block * r, 0.0)
        inverse[g] = jnp.where(cols <= rows + o, s[g] * r, 0.0)
    return jnp.concatenate(upper, 0), jnp.concatenate(inverse, 0)


def factor_tile(w_ref, l_ref, v_ref):
    v_ref[...] = jnp.zeros((TILE, TILE), F32)
    l_ref[...] = jnp.zeros((TILE, TILE), F32)

    def step(b, carry):
        off = pl.multiple_of(b * NB, NB)
        ub, vb = block_factor([w_ref[pl.ds(off + 8 * i, 8), pl.ds(off, NB)] for i in range(16)])
        lb = ub.T
        for bb in range(NBLK):

            @pl.when(b == bb)
            def _(bb=bb):
                o = bb * NB
                e = o + NB
                l_ref[o:e, o:e] = lb
                if bb > 0:
                    v_ref[o:e, :o] = jnp.dot(vb, v_ref[o:e, :o], precision=HIGHEST, preferred_element_type=F32)
                v_ref[o:e, o:e] = vb
                if bb < NBLK - 1:
                    lp = times_t(w_ref[e:, o:e], vb)
                    l_ref[e:, o:e] = lp
                    w_ref[e:, e:] -= times_t(lp, lp)
                    v_ref[e:, :e] -= jnp.dot(lp, v_ref[o:e, :e], precision=HIGHEST, preferred_element_type=F32)

        return carry

    lax.fori_loop(0, NBLK, step, 0)


def assemble(dst_ref, mine_ref, other_ref, t, where_ref):
    y, core = where_ref[0], where_ref[1]
    for m in range(4):
        at = lax.rem(y + 4 - m, 4) * 2
        for src, k in ((mine_ref, core), (other_ref, 1 - core)):
            dst_ref[pl.ds(pl.multiple_of((at + k) * PART, PART), PART), :] = src[m, t]


def first_kernel(where_ref, mine_ref, other_ref, l_ref, v_ref, w_ref):
    assemble(w_ref, mine_ref, other_ref, 0, where_ref)
    factor_tile(w_ref, l_ref, v_ref)


def factor_first(where, mine, other):
    return pl.pallas_call(
        first_kernel,
        out_shape=square(2),
        in_specs=[SMEM, VMEM, VMEM],
        out_specs=(VMEM,) * 2,
        scratch_shapes=[pltpu.VMEM((TILE, TILE), F32)],
        cost_estimate=pl.CostEstimate(flops=10**10, bytes_accessed=3 << 20, transcendentals=0),
        name="factor_first",
    )(where, mine, other)


def second_kernel(where_ref, mine_ref, other_ref, v0_ref, p_ref, l_ref, v_ref, w_ref):
    assemble(w_ref, mine_ref, other_ref, 0, where_ref)
    p_ref[...] = times_t(w_ref[...], v0_ref[...])
    assemble(w_ref, mine_ref, other_ref, 1, where_ref)
    w_ref[...] -= times_t(p_ref[...], p_ref[...])
    factor_tile(w_ref, l_ref, v_ref)


def factor_second(where, mine, other, inverse0):
    return pl.pallas_call(
        second_kernel,
        out_shape=square(3),
        in_specs=[SMEM, VMEM, VMEM, VMEM],
        out_specs=(VMEM,) * 3,
        scratch_shapes=[pltpu.VMEM((TILE, TILE), F32)],
        cost_estimate=pl.CostEstimate(flops=10**10, bytes_accessed=6 << 20, transcendentals=0),
        name="factor_second",
    )(where, mine, other, inverse0)


def split(v):
    hi = v.astype(jnp.bfloat16)
    return hi, (v - hi.astype(F32)).astype(jnp.bfloat16)


def times_t3(a, b):
    def one(p, q):
        return lax.dot_general(p, q, (((1,), (1,)), ((), ())), preferred_element_type=F32)

    return one(a[0], b[0]) + (one(a[0], b[1]) + one(a[1], b[0]))


def prepare_kernel(where_ref, mine_ref, other_ref, v0_ref, p01_ref, v1_ref, p0_ref, p1_ref, w_ref):
    assemble(w_ref, mine_ref, other_ref, 2, where_ref)
    p0 = times_t3(split(w_ref[...]), split(v0_ref[...]))
    p0_ref[...] = p0
    assemble(w_ref, mine_ref, other_ref, 3, where_ref)
    next1 = w_ref[...] - times_t3(split(p0), split(p01_ref[...]))
    p1_ref[...] = times_t3(split(next1), split(v1_ref[...]))


def prepare(where, mine, other, inverse0, p01, inverse1):
    return pl.pallas_call(
        prepare_kernel,
        out_shape=square(2),
        in_specs=[SMEM] + [VMEM] * 5,
        out_specs=(VMEM,) * 2,
        scratch_shapes=[pltpu.VMEM((TILE, TILE), F32)],
        cost_estimate=pl.CostEstimate(flops=3 * 10**9, bytes_accessed=9 << 20, transcendentals=0),
        name="prepare",
    )(where, mine, other, inverse0, p01, inverse1)


UPDATE_BOTH, UPDATE_SECOND, KEEP, PANEL0, PANEL1, LATE_PANEL1, FACTOR0, FACTOR1 = range(8)


HALF = TILE // 2


def finish_kernel(at_ref, kind_ref, raw_ref, a_ref, v0, p01, v1, p0j, p1j, f0, f1, o_ref, w_ref):
    kind = kind_ref[pl.program_id(0)]

    @pl.when((pl.program_id(0) == 0) & (pl.program_id(1) == 0))
    def _():
        for n, ref in enumerate((v0, p01, v1, p0j, p1j)):
            hi, lo = split(ref[...])
            w_ref[n] = jnp.concatenate([hi, lo, hi], 1)

    def times(v, n):
        hi, lo = split(v)
        return lax.dot_general(
            jnp.concatenate([hi, hi, lo], 1), w_ref[n], (((1,), (1,)), ((), ())), preferred_element_type=F32
        )

    def raw(t):
        return raw_ref[:, t].reshape(HALF, TILE)

    @pl.when(kind == UPDATE_BOTH)
    def _():
        p0 = times(raw(0), 0)
        p1 = times(raw(1) - times(p0, 1), 2)
        o_ref[0] = a_ref[0] - times(p0, 3) - times(p1, 4)

    @pl.when(kind == UPDATE_SECOND)
    def _():
        o_ref[0] = a_ref[0] - times(times(raw(1), 2), 4)

    @pl.when(kind == PANEL0)
    def _():
        o_ref[0] = times(raw(0), 0)

    @pl.when(kind == PANEL1)
    def _():
        p0 = times(raw(0), 0)
        o_ref[0] = times(raw(1) - times(p0, 1), 2)

    @pl.when(kind == LATE_PANEL1)
    def _():
        o_ref[0] = times(raw(1), 2)

    @pl.when(kind == KEEP)
    def _():
        o_ref[...] = a_ref[...]

    @pl.when(kind == FACTOR0)
    def _():
        o_ref[0] = f0[...]

    @pl.when(kind == FACTOR1)
    def _():
        o_ref[0] = f1[...]


def finish(at, kind, panels, local, inverse0, p01, inverse1, p0j, p1j, factor0, factor1):
    whole = pl.BlockSpec((TILE, TILE), lambda s, h, at, kind: (0, 0))
    tile = pl.BlockSpec((1, HALF, TILE), lambda s, h, at, kind: (s, h, 0))
    half = pl.BlockSpec((HALF, TILE), lambda s, h, at, kind: (h, 0))
    return pl.pallas_call(
        finish_kernel,
        out_shape=jax.ShapeDtypeStruct(local.shape, F32),
        grid_spec=pltpu.PrefetchScalarGridSpec(
            num_scalar_prefetch=2,
            grid=(local.shape[0], 2),
            in_specs=[pl.BlockSpec((4, 2, PART, TILE), lambda s, h, at, kind: (2 * at[s] + h, 0, 0, 0)), tile]
            + [whole] * 5
            + [half] * 2,
            out_specs=tile,
            scratch_shapes=[pltpu.VMEM((5, TILE, 3 * TILE), jnp.bfloat16)],
        ),
        cost_estimate=pl.CostEstimate(flops=3 * 10**10, bytes_accessed=24 << 20, transcendentals=0),
        name="finish",
    )(at, kind, panels, local, inverse0, p01, inverse1, p0j, p1j, factor0, factor1)


BANDT = 32
ROWS = 8
COLS = 32
AX = ("row", "col")


def lin(r, c):
    return (r % ROWS) * COLS + c % COLS


def zx(z, x):
    return (z % 8) * 4 + x % 4


def permute(v, pairs):
    return lax.ppermute(v, AX, [(lin(*a), lin(*b)) for a, b in pairs])


EVERY = [(r, z, x) for r in range(ROWS) for z in range(8) for x in range(4)]


def core_swap(v):
    return permute(v, [((r, zx(z, x)), (r ^ 1, zx(z, x))) for r, z, x in EVERY])


def y_shift(v, k):
    return permute(v, [((r, zx(z, x)), (r + 2 * k, zx(z, x))) for r, z, x in EVERY])


def x_deal(v, k):
    return permute(v, [((r, zx(z, x)), (r, zx(z, x + k))) for r, z, x in EVERY if x < 2])


def z_deal(v, k):
    return permute(v, [((r, zx(0, x)), (r, zx(k, x))) for r, z, x in EVERY if z == 0 and x < 2])


def pick(choices):
    total = None
    for cond, v in choices:
        v = jnp.where(cond, v, 0.0)
        total = v if total is None else total + v
    return total


def spread_x(v, x):
    got = permute(v, [((r, zx(0, 0)), (r, zx(0, 2))) for r in range(ROWS)])
    v = jnp.where(x == 2, got, v)
    got = permute(v, [((r, zx(0, a)), (r, zx(0, a + 1))) for r in range(ROWS) for a in (0, 2)])
    return jnp.where(x % 2 == 1, got, v)


def spread_z(v, z, steps):
    for step in steps:
        pairs = [((r, zx(a, b)), (r, zx(a + step, b))) for r in range(ROWS) for a in range(0, 8, 2 * step) for b in range(4)]
        got = permute(v, pairs)
        v = jnp.where(z % (2 * step) == step, got, v)
    return v


def ring(piece):
    return [piece] + [y_shift(piece, m) for m in range(1, 4)]


def with_partner(pieces):
    mine = jnp.stack(pieces)
    return mine, core_swap(mine)


def shards(band):
    slots, _, _, _, tile, _ = band.shape
    part = tile // ROWS
    row = lax.axis_index("row")
    col = lax.axis_index("col")
    z, x = col // 4, col % 4
    y, core = row // 2, row % 2
    local = band.reshape(slots, tile, tile)
    where = jnp.stack([y, core]).astype(jnp.int32)

    eighths = local.reshape(8, slots * tile // 8, tile)
    skip = jnp.where((row == 0) & (x == 1), 6, 0)

    def eighth(k):
        return lax.dynamic_index_in_dim(eighths, (skip + k) % 8, 0, keepdims=False)

    arrived = [z_deal(eighth(k), k) for k in range(1, 8)]

    partner = core_swap(local[0])
    even = jnp.where(core == 0, local[0], partner).reshape(4, 2, part, tile)
    odd = jnp.where(core == 0, partner, local[0]).reshape(4, 2, part, tile)
    both = jnp.stack([even, odd], 1)
    both = lax.dynamic_index_in_dim(both, core, 2, keepdims=False)
    mine = [(y == 0, both[0])] + [(y == k, y_shift(both[k], k)) for k in range(1, 4)]
    mine = pick(mine)
    first = spread_z(spread_x(mine[:1], x), z, (4,))
    beside = permute(mine[1], [((r, 1), (r, 0)) for r in range(ROWS)])
    second = spread_x(jnp.stack([mine[1], beside]), x)
    first, second, arrived = lax.optimization_barrier((first, second, arrived))
    first = spread_z(first, z, (2,))
    first, second = spread_z(first, z, (1,)), spread_z(second, z, (4, 2, 1))
    first = with_partner(ring(first))

    dealt = pick([(z == 0, eighth(0))] + [(z == k, arrived[k - 1]) for k in range(1, 8)])
    fourths = dealt.reshape(4, part, tile)
    p0, p1 = [(x == 0, fourths[0])], [(x == 1, fourths[1])]
    for k in range(1, 4):
        got = x_deal(jnp.where(x == 0, fourths[k], fourths[(k + 1) % 4]), k)
        p0.append((x == k, got))
        p1.append((x == (k + 1) % 4, got))
    piece = jnp.stack([pick(p0), pick(p1)])
    panels = lax.all_gather(piece, "col")

    pairs = [((r, 8 * s + q), (q, 8 * s + r)) for s in range(slots) for r in range(ROWS) for q in range(ROWS)]
    crossed = permute(piece, pairs)
    factor0, inverse0 = factor_first(where, *first)
    inverse0, second, crossed = lax.optimization_barrier((inverse0, second, crossed))
    rest = with_partner(ring(jnp.concatenate([second, crossed])))
    p01, factor1, inverse1 = factor_second(where, *rest, inverse0)
    p0j, p1j = prepare(where, *rest, inverse0, p01, inverse1)

    rows_here = col + (row - col) % ROWS + ROWS * jnp.arange(slots, dtype=jnp.int32)
    at = (rows_here // ROWS) % slots
    update = jnp.where(rows_here < BANDT, UPDATE_BOTH, jnp.where(rows_here == BANDT, UPDATE_SECOND, KEEP))
    panel0 = jnp.where(rows_here == 0, FACTOR0, PANEL0)
    panel1 = jnp.where(rows_here == 1, FACTOR1, jnp.where(rows_here == BANDT, LATE_PANEL1, PANEL1))
    kind = jnp.where(col == 0, panel0, jnp.where(col == 1, panel1, update)).astype(jnp.int32)
    out = finish(at, kind, panels, local, inverse0, p01, inverse1, p0j, p1j, factor0, factor1)
    return out.reshape(band.shape)


def solution(mesh):
    spec = P(None, "row", None, "col", None, None)

    return jax.shard_map(shards, mesh=mesh, in_specs=(spec,), out_specs=spec, check_vma=False)
```

```python
import jax
import jax.numpy as jnp
from jax import lax
from jax.experimental import pallas as pl
from jax.experimental.pallas import tpu as pltpu
from jax.sharding import PartitionSpec as P


TILE = 512
NB = 128
NBLK = TILE // NB
PART = TILE // 8
HIGHEST = lax.Precision.HIGHEST
VMEM = pl.BlockSpec(memory_space=pltpu.VMEM)
SMEM = pl.BlockSpec(memory_space=pltpu.SMEM)
F32 = jnp.float32


def square(n=1):
    return (jax.ShapeDtypeStruct((TILE, TILE), F32),) * n


def times_t(a, b):
    return lax.dot_general(a, b, (((1,), (1,)), ((), ())), precision=HIGHEST, preferred_element_type=F32)


def block_factor(s):
    rows = lax.broadcasted_iota(jnp.int32, (8, NB), 0)
    cols = lax.broadcasted_iota(jnp.int32, (8, NB), 1)

    def lane(v, c):
        return jnp.broadcast_to(v[:, c : c + 1], (8, NB))

    def sub(v, j):
        return jnp.broadcast_to(v[j : j + 1, :], (8, NB))

    upper, inverse = [None] * 16, [None] * 16
    for g in range(16):
        o = 8 * g
        inside = (cols >= o) & (cols < o + 8)
        c = [lane(s[g], o + k) for k in range(8)]
        s[g] = jnp.where(inside, jnp.where(cols == rows + o, 1.0, 0.0), s[g])
        inv, q, sr = [None] * 8, [[None] * 8 for _ in range(8)], [None] * 8
        pivots = None
        for k in range(8):
            piv = sub(c[k], k)
            pivots = piv if k == 0 else jnp.where(rows == k, piv, pivots)
            inv[k] = 1.0 / piv
            sr[k] = sub(s[g], k)
            if k < 7:
                t = jnp.where(rows > k, c[k] * inv[k], 0.0)
                for k2 in range(k + 1, 8):
                    q[k][k2] = sub(c[k2], k)
                    c[k2] = c[k2] - t * q[k][k2]
                s[g] = s[g] - t * sr[k]
        for i in range(g + 1, 16):
            ci = [lane(s[i], o + k) for k in range(8)]
            s[i] = jnp.where(inside, 0.0, s[i])
            for k in range(8):
                t = ci[k] * inv[k]
                for k2 in range(k + 1, 8):
                    ci[k2] = ci[k2] - t * q[k][k2]
                s[i] = s[i] - t * sr[k]
        block = s[g]
        for k in range(8):
            block = jnp.where(cols == o + k, c[k], block)
        r = lax.rsqrt(pivots)
        upper[g] = jnp.where(cols >= rows + o, block * r, 0.0)
        inverse[g] = jnp.where(cols <= rows + o, s[g] * r, 0.0)
    return jnp.concatenate(upper, 0), jnp.concatenate(inverse, 0)


def factor_tile(w_ref, l_ref, v_ref):
    v_ref[...] = jnp.zeros((TILE, TILE), F32)
    l_ref[...] = jnp.zeros((TILE, TILE), F32)

    def step(b, carry):
        off = pl.multiple_of(b * NB, NB)
        ub, vb = block_factor([w_ref[pl.ds(off + 8 * i, 8), pl.ds(off, NB)] for i in range(16)])
        lb = ub.T
        for bb in range(NBLK):

            @pl.when(b == bb)
            def _(bb=bb):
                o = bb * NB
                e = o + NB
                l_ref[o:e, o:e] = lb
                if bb > 0:
                    v_ref[o:e, :o] = jnp.dot(vb, v_ref[o:e, :o], precision=HIGHEST, preferred_element_type=F32)
                v_ref[o:e, o:e] = vb
                if bb < NBLK - 1:
                    lp = times_t(w_ref[e:, o:e], vb)
                    l_ref[e:, o:e] = lp
                    w_ref[e:, e:] -= times_t(lp, lp)
                    v_ref[e:, :e] -= jnp.dot(lp, v_ref[o:e, :e], precision=HIGHEST, preferred_element_type=F32)

        return carry

    lax.fori_loop(0, NBLK, step, 0)


def assemble(dst_ref, mine_ref, other_ref, t, where_ref):
    y, core = where_ref[0], where_ref[1]
    for m in range(4):
        at = lax.rem(y + 4 - m, 4) * 2
        for src, k in ((mine_ref, core), (other_ref, 1 - core)):
            dst_ref[pl.ds(pl.multiple_of((at + k) * PART, PART), PART), :] = src[m, t]


def first_kernel(where_ref, mine_ref, other_ref, l_ref, v_ref, w_ref):
    assemble(w_ref, mine_ref, other_ref, 0, where_ref)
    factor_tile(w_ref, l_ref, v_ref)


def factor_first(where, mine, other):
    return pl.pallas_call(
        first_kernel,
        out_shape=square(2),
        in_specs=[SMEM, VMEM, VMEM],
        out_specs=(VMEM,) * 2,
        scratch_shapes=[pltpu.VMEM((TILE, TILE), F32)],
        cost_estimate=pl.CostEstimate(flops=10**10, bytes_accessed=3 << 20, transcendentals=0),
        name="factor_first",
    )(where, mine, other)


def second_kernel(where_ref, mine_ref, other_ref, v0_ref, p_ref, l_ref, v_ref, w_ref):
    assemble(w_ref, mine_ref, other_ref, 0, where_ref)
    p_ref[...] = times_t(w_ref[...], v0_ref[...])
    assemble(w_ref, mine_ref, other_ref, 1, where_ref)
    w_ref[...] -= times_t(p_ref[...], p_ref[...])
    factor_tile(w_ref, l_ref, v_ref)


def factor_second(where, mine, other, inverse0):
    return pl.pallas_call(
        second_kernel,
        out_shape=square(3),
        in_specs=[SMEM, VMEM, VMEM, VMEM],
        out_specs=(VMEM,) * 3,
        scratch_shapes=[pltpu.VMEM((TILE, TILE), F32)],
        cost_estimate=pl.CostEstimate(flops=10**10, bytes_accessed=6 << 20, transcendentals=0),
        name="factor_second",
    )(where, mine, other, inverse0)


def split(v):
    hi = v.astype(jnp.bfloat16)
    return hi, (v - hi.astype(F32)).astype(jnp.bfloat16)


def times_t3(a, b):
    def one(p, q):
        return lax.dot_general(p, q, (((1,), (1,)), ((), ())), preferred_element_type=F32)

    return one(a[0], b[0]) + (one(a[0], b[1]) + one(a[1], b[0]))


def product3(a, b):
    def one(p, q):
        return jnp.dot(p, q, preferred_element_type=F32)

    return one(a[0], b[0]) + (one(a[0], b[1]) + one(a[1], b[0]))


def prepare_kernel(where_ref, mine_ref, other_ref, v0_ref, p01_ref, v1_ref, t0_ref, t1_ref, w_ref):
    assemble(w_ref, mine_ref, other_ref, 2, where_ref)
    v0, p01, v1 = split(v0_ref[...]), split(p01_ref[...]), split(v1_ref[...])
    p0 = times_t3(split(w_ref[...]), v0)
    assemble(w_ref, mine_ref, other_ref, 3, where_ref)
    p1 = times_t3(split(w_ref[...] - times_t3(split(p0), p01)), v1)
    t1 = product3(split(p1), v1)
    t1_ref[...] = t1
    t0_ref[...] = product3(split(p0 - product3(split(t1), p01)), v0)


def prepare(where, mine, other, inverse0, p01, inverse1):
    return pl.pallas_call(
        prepare_kernel,
        out_shape=square(2),
        in_specs=[SMEM] + [VMEM] * 5,
        out_specs=(VMEM,) * 2,
        scratch_shapes=[pltpu.VMEM((TILE, TILE), F32)],
        cost_estimate=pl.CostEstimate(flops=3 * 10**9, bytes_accessed=9 << 20, transcendentals=0),
        name="prepare",
    )(where, mine, other, inverse0, p01, inverse1)


UPDATE_BOTH, UPDATE_SECOND, KEEP, PANEL0, PANEL1, LATE_PANEL1, FACTOR0, FACTOR1 = range(8)


HALF = TILE // 2


def finish_kernel(at_ref, kind_ref, raw_ref, a_ref, v0, p01, v1, p0j, p1j, f0, f1, o_ref, w_ref):
    kind = kind_ref[pl.program_id(0)]

    @pl.when((pl.program_id(0) == 0) & (pl.program_id(1) == 0))
    def _():
        for n, ref in enumerate((v0, p01, v1, p0j, p1j)):
            hi, lo = split(ref[...])
            w_ref[n] = jnp.concatenate([hi, lo, hi], 1)

    def times(v, n):
        hi, lo = split(v)
        return lax.dot_general(
            jnp.concatenate([hi, hi, lo], 1), w_ref[n], (((1,), (1,)), ((), ())), preferred_element_type=F32
        )

    def raw(t):
        return raw_ref[:, t].reshape(HALF, TILE)

    @pl.when(kind == UPDATE_BOTH)
    def _():
        o_ref[0] = a_ref[0] - times(raw(0), 3) - times(raw(1), 4)

    @pl.when(kind == UPDATE_SECOND)
    def _():
        o_ref[0] = a_ref[0] - times(raw(1), 4)

    @pl.when(kind == PANEL0)
    def _():
        o_ref[0] = times(raw(0), 0)

    @pl.when(kind == PANEL1)
    def _():
        p0 = times(raw(0), 0)
        o_ref[0] = times(raw(1) - times(p0, 1), 2)

    @pl.when(kind == LATE_PANEL1)
    def _():
        o_ref[0] = times(raw(1), 2)

    @pl.when(kind == KEEP)
    def _():
        o_ref[...] = a_ref[...]

    @pl.when(kind == FACTOR0)
    def _():
        o_ref[0] = f0[...]

    @pl.when(kind == FACTOR1)
    def _():
        o_ref[0] = f1[...]


def finish(at, kind, panels, local, inverse0, p01, inverse1, p0j, p1j, factor0, factor1):
    whole = pl.BlockSpec((TILE, TILE), lambda s, h, at, kind: (0, 0))
    tile = pl.BlockSpec((1, HALF, TILE), lambda s, h, at, kind: (s, h, 0))
    half = pl.BlockSpec((HALF, TILE), lambda s, h, at, kind: (h, 0))
    return pl.pallas_call(
        finish_kernel,
        out_shape=jax.ShapeDtypeStruct(local.shape, F32),
        grid_spec=pltpu.PrefetchScalarGridSpec(
            num_scalar_prefetch=2,
            grid=(local.shape[0], 2),
            in_specs=[pl.BlockSpec((4, 2, PART, TILE), lambda s, h, at, kind: (2 * at[s] + h, 0, 0, 0)), tile]
            + [whole] * 5
            + [half] * 2,
            out_specs=tile,
            scratch_shapes=[pltpu.VMEM((5, TILE, 3 * TILE), jnp.bfloat16)],
        ),
        cost_estimate=pl.CostEstimate(flops=3 * 10**10, bytes_accessed=24 << 20, transcendentals=0),
        name="finish",
    )(at, kind, panels, local, inverse0, p01, inverse1, p0j, p1j, factor0, factor1)


BANDT = 32
ROWS = 8
COLS = 32
AX = ("row", "col")


def lin(r, c):
    return (r % ROWS) * COLS + c % COLS


def zx(z, x):
    return (z % 8) * 4 + x % 4


def permute(v, pairs):
    return lax.ppermute(v, AX, [(lin(*a), lin(*b)) for a, b in pairs])


EVERY = [(r, z, x) for r in range(ROWS) for z in range(8) for x in range(4)]


def core_swap(v):
    return permute(v, [((r, zx(z, x)), (r ^ 1, zx(z, x))) for r, z, x in EVERY])


def y_shift(v, k):
    return permute(v, [((r, zx(z, x)), (r + 2 * k, zx(z, x))) for r, z, x in EVERY])


def x_deal(v, k):
    return permute(v, [((r, zx(z, x)), (r, zx(z, x + k))) for r, z, x in EVERY if x < 2])


def z_deal(v, k):
    return permute(v, [((r, zx(0, x)), (r, zx(k, x))) for r, z, x in EVERY if z == 0 and x < 2])


def pick(choices):
    total = None
    for cond, v in choices:
        v = jnp.where(cond, v, 0.0)
        total = v if total is None else total + v
    return total


def spread_x(v, x):
    got = permute(v, [((r, zx(0, 0)), (r, zx(0, 2))) for r in range(ROWS)])
    v = jnp.where(x == 2, got, v)
    got = permute(v, [((r, zx(0, a)), (r, zx(0, a + 1))) for r in range(ROWS) for a in (0, 2)])
    return jnp.where(x % 2 == 1, got, v)


def spread_z(v, z, steps):
    for step in steps:
        pairs = [((r, zx(a, b)), (r, zx(a + step, b))) for r in range(ROWS) for a in range(0, 8, 2 * step) for b in range(4)]
        got = permute(v, pairs)
        v = jnp.where(z % (2 * step) == step, got, v)
    return v


def ring(piece):
    return [piece] + [y_shift(piece, m) for m in range(1, 4)]


def with_partner(pieces):
    mine = jnp.stack(pieces)
    return mine, core_swap(mine)


def shards(band):
    slots, _, _, _, tile, _ = band.shape
    part = tile // ROWS
    row = lax.axis_index("row")
    col = lax.axis_index("col")
    z, x = col // 4, col % 4
    y, core = row // 2, row % 2
    local = band.reshape(slots, tile, tile)
    where = jnp.stack([y, core]).astype(jnp.int32)

    eighths = local.reshape(8, slots * tile // 8, tile)
    skip = jnp.where((row == 0) & (x == 1), 6, 0)

    def eighth(k):
        return lax.dynamic_index_in_dim(eighths, (skip + k) % 8, 0, keepdims=False)

    arrived = [z_deal(eighth(k), k) for k in range(1, 8)]

    partner = core_swap(local[0])
    even = jnp.where(core == 0, local[0], partner).reshape(4, 2, part, tile)
    odd = jnp.where(core == 0, partner, local[0]).reshape(4, 2, part, tile)
    both = jnp.stack([even, odd], 1)
    both = lax.dynamic_index_in_dim(both, core, 2, keepdims=False)
    mine = [(y == 0, both[0])] + [(y == k, y_shift(both[k], k)) for k in range(1, 4)]
    mine = pick(mine)
    first = spread_z(spread_x(mine[:1], x), z, (4,))
    beside = permute(mine[1], [((r, 1), (r, 0)) for r in range(ROWS)])
    second = spread_x(jnp.stack([mine[1], beside]), x)
    first, second, arrived = lax.optimization_barrier((first, second, arrived))
    first, second = spread_z(first, z, (2, 1)), spread_z(second, z, (4, 2, 1))
    first = with_partner(ring(first))

    dealt = pick([(z == 0, eighth(0))] + [(z == k, arrived[k - 1]) for k in range(1, 8)])
    fourths = dealt.reshape(4, part, tile)
    p0, p1 = [(x == 0, fourths[0])], [(x == 1, fourths[1])]
    for k in range(1, 4):
        got = x_deal(jnp.where(x == 0, fourths[k], fourths[(k + 1) % 4]), k)
        p0.append((x == k, got))
        p1.append((x == (k + 1) % 4, got))
    piece = jnp.stack([pick(p0), pick(p1)])
    panels = lax.all_gather(piece, "col")

    pairs = [((r, 8 * s + q), (q, 8 * s + r)) for s in range(slots) for r in range(ROWS) for q in range(ROWS)]
    rest = ring(jnp.concatenate([second, permute(piece, pairs)]))
    factor0, inverse0 = factor_first(where, *first)
    inverse0, rest = lax.optimization_barrier((inverse0, rest))
    rest = with_partner(rest)
    p01, factor1, inverse1 = factor_second(where, *rest, inverse0)
    p0j, p1j = prepare(where, *rest, inverse0, p01, inverse1)

    rows_here = col + (row - col) % ROWS + ROWS * jnp.arange(slots, dtype=jnp.int32)
    at = (rows_here // ROWS) % slots
    update = jnp.where(rows_here < BANDT, UPDATE_BOTH, jnp.where(rows_here == BANDT, UPDATE_SECOND, KEEP))
    panel0 = jnp.where(rows_here == 0, FACTOR0, PANEL0)
    panel1 = jnp.where(rows_here == 1, FACTOR1, jnp.where(rows_here == BANDT, LATE_PANEL1, PANEL1))
    kind = jnp.where(col == 0, panel0, jnp.where(col == 1, panel1, update)).astype(jnp.int32)
    out = finish(at, kind, panels, local, inverse0, p01, inverse1, p0j, p1j, factor0, factor1)
    return out.reshape(band.shape)


def solution(mesh):
    spec = P(None, "row", None, "col", None, None)

    return jax.shard_map(shards, mesh=mesh, in_specs=(spec,), out_specs=spec, check_vma=False)
```
